512 devices in a mesh: dp: 32 (over y, x), tm: 16 (over z, core).
Axes of the slice: x: 4, y: 8, z: 8, core: 2. Of those that a mesh axis runs over, the one named last changes fastest.
Arguments:
- tokens: bfloat16 [32, 16, 256, 1024], P('dp', 'tm'), may hold values from -6 to 6
- gain: bfloat16 [1024], replicated, may hold values from 0.25 to 1.75
- w_qkv: bfloat16 [1024, 3072], P('dp'), may hold values from -0.1875 to 0.1875
- w_out: bfloat16 [1024, 1024], P('dp'), may hold values from -0.1875 to 0.1875
- w_pair: float32 [2, 1024, 32], replicated, may hold values from -3 to 3
- codebook: float32 [8, 32], replicated, may hold values from -5 to 5
- codes: int32 [32, 16, 1], P('dp', 'tm'), may hold values from 0 to 7
Outputs:
- grad_tokens: bfloat16 [32, 16, 256, 1024], P('dp', 'tm')
- grad_pair: float32 [2, 1024, 32], replicated
- codebook_step: float32 [8, 32], replicated
The draws below stay inside these ranges and needn't reach their ends.
Inputs may be any that keep to these rules, and one draw needn't show every extreme that they name: Every one of the 8 codes is assigned to some clip frame.
All inputs are finite; a program needn't handle non-finite values.
Results may differ from the reference program's by a relative error of at most 0.014.
Values may be sent and summed in bfloat16 or wider, within the bound.
No kernel may reach another device: no remote copies, remote signals or barrier semaphores. Data moves between devices by JAX's collectives and lax.ppermute only.
A program may use at most 64 MiB of HBM per device.

```python
import jax
import jax.numpy as jnp
from jax import lax

D = 1024
HEAD_DIM = 64
LATENT = 32
CODES = 8
PATCHES = 256
CLIPS = 32
FRAMES = 16


def levels(rng, dims, pieces, least, top_value):
    loudness, own = 1.0, jax.random.fold_in(rng, 6)
    for dim, blocks in pieces:
        heights = jnp.exp(jax.random.uniform(jax.random.fold_in(own, dim), (blocks,), jnp.float32, least / len(pieces), top_value / len(pieces)))
        loudness = loudness * jnp.repeat(heights, dims[dim] // blocks).reshape([-1 if axis == dim else 1 for axis in range(len(dims))])
    return loudness


def distinct(key, rows, number_of, top, lift):
    ranking = jax.random.permutation(jax.random.fold_in(key, 1), number_of)
    favour = ranking
    for power in range(3):
        favour = favour * favour // number_of
    favour = favour * lift // number_of
    chance = jax.random.randint(jax.random.fold_in(key, 2), (rows, number_of), 0, 4096) + favour
    holders = jax.random.permutation(jax.random.fold_in(key, 3), rows)[jnp.arange(number_of) % rows]
    chance = jnp.where(jnp.arange(rows)[:, None] == holders[None, :], 1 << 14, chance)
    priority = chance * number_of + jnp.arange(number_of)
    return lax.top_k(priority.astype(jnp.int32), top)[1].astype(jnp.int32)


def scatter_about(own_key, dims, scale, bound, split=(), held_as=jnp.bfloat16):
    result = scale * jax.random.normal(own_key, dims, jnp.float32)
    if split:
        result = result * levels(own_key, dims, split, -0.22, 0.18)
    return jnp.clip(result, -bound, bound).astype(held_as)


def setup_inputs(seed: int = 0) -> dict:
    splits = jax.random.split(jax.random.key(seed), 8)
    return {
        "tokens": scatter_about(splits[0], (CLIPS, FRAMES, PATCHES, D), 1.0, 6.0, ((0, 32), (1, 16))),
        "gain": jnp.clip(1.0 + 0.15 * jax.random.normal(splits[1], (D,), jnp.float32), 0.25, 1.75).astype(jnp.bfloat16),
        "w_qkv": scatter_about(splits[2], (D, 3 * D), D ** -0.5, 0.1875, ((0, 32),)),
        "w_out": scatter_about(splits[3], (D, D), D ** -0.5, 0.1875, ((0, 32),)),
        "w_pair": scatter_about(splits[4], (2, D, LATENT), (D // PATCHES) ** -0.5, 3.0, (), jnp.float32),
        "codebook": scatter_about(splits[5], (CODES, LATENT), 1.0, 5.0, (), jnp.float32),
        "codes": distinct(splits[6], CLIPS * FRAMES, CODES, 1, 1024).reshape((CLIPS, FRAMES, 1)),
    }


EPS = 1e-06
BETA = 0.25

def normalize(xf, gain):
    scale = lax.rsqrt(lax.optimization_barrier(jnp.mean(xf * xf, axis=-1, keepdims=True)) + EPS)
    return (xf * scale * gain.astype(jnp.float32)).astype(jnp.bfloat16)

def project(normed, weight):
    shape = normed.shape
    flat = jnp.dot(normed.reshape(-1, shape[-1]), weight, preferred_element_type=jnp.float32)
    return flat.astype(jnp.bfloat16).reshape(shape[:-1] + (3, shape[-1]))

def attend(qkv):
    clips, frames, patches, _, width = qkv.shape
    local_heads = width // HEAD_DIM
    parts = qkv.reshape(clips, frames, patches, 3, local_heads, HEAD_DIM)
    query = parts[:, :, :, 0].astype(jnp.float32)
    keys = parts[:, :, :, 1].astype(jnp.float32)
    values = parts[:, :, :, 2].astype(jnp.float32)
    scores = jnp.einsum('cfphd,cgphd->cphfg', query, keys) * HEAD_DIM ** (-0.5)
    causal = jnp.arange(frames)[:, None] >= jnp.arange(frames)[None, :]
    scores = jnp.where(causal, scores, -1e+30)
    weights = jax.nn.softmax(scores, axis=-1).astype(jnp.bfloat16)
    mixed = jnp.einsum('cphfg,cgphd->cfphd', weights.astype(jnp.float32), values)
    return mixed.reshape(clips, frames, patches, width).astype(jnp.bfloat16)

def output(xf, attended, weight):
    shape = xf.shape
    moved = jnp.dot(attended.reshape(-1, shape[-1]), weight, preferred_element_type=jnp.float32)
    return lax.optimization_barrier(jnp.mean(xf + moved.reshape(shape), axis=2))

def reference(tokens, gain, w_qkv, w_out, w_pair, codebook, codes):

    def whole(xf):
        return output(xf, attend(project(normalize(xf, gain), w_qkv)), w_out)

    def forward(clip):
        return whole(clip[None].astype(jnp.float32))[0]
    pooled = lax.map(forward, tokens)
    following = jnp.concatenate([pooled[:, 1:], jnp.zeros_like(pooled[:, :1])], axis=1)
    flat_now = pooled.reshape(-1, D)
    flat_next = following.reshape(-1, D)
    hp = lax.Precision.HIGHEST
    action = jnp.dot(flat_now, w_pair[0], precision=hp) + jnp.dot(flat_next, w_pair[1], precision=hp)
    onehot = (codes.reshape(-1)[:, None] == jnp.arange(CODES)[None, :]).astype(jnp.float32)
    quantized = jnp.dot(onehot, codebook, precision=hp)
    diff = action - quantized
    d_action = 2.0 * BETA * diff
    d_quant = -2.0 * diff
    count = lax.optimization_barrier(jnp.sum(onehot, axis=0))
    codebook_step = jnp.dot(onehot.T, d_quant, precision=hp) / count[:, None]
    grad_pair = jnp.stack([jnp.dot(flat_now.T, d_action, precision=hp), jnp.dot(flat_next.T, d_action, precision=hp)])
    d_own = jnp.dot(d_action, w_pair[0].T, precision=hp).reshape(pooled.shape)
    d_next = jnp.dot(d_action, w_pair[1].T, precision=hp).reshape(pooled.shape)
    carried = jnp.concatenate([jnp.zeros_like(d_next[:, :1]), d_next[:, :-1]], axis=1)
    d_pooled = (d_own + carried) * PATCHES

    def backward(pair):
        clip, cotangent = pair
        _, pull = jax.vjp(whole, clip[None].astype(jnp.float32))
        return pull(cotangent[None])[0][0].astype(jnp.bfloat16)
    grad_tokens = lax.map(backward, (tokens, d_pooled))
    return (grad_tokens, grad_pair, codebook_step)
```

```python
import jax
import jax.numpy as jnp
from jax import lax
from jax.experimental import pallas as pl
from jax.experimental.pallas import tpu as pltpu
from jax.sharding import Mesh
from jax.sharding import PartitionSpec as P

D = 1024
HEAD_DIM = 64
LATENT = 32
CODES = 8
PATCHES = 256
FRAMES = 16
EPS = 1e-06
BETA = 0.25
DP = ("dp_0", "dp_1")
TM = ("tm_0", "tm_1")
HALF = 512
EXTRA = 256
GRADS = 512
PIECES = 5
BF = jnp.bfloat16
F32 = jnp.float32
HIGHEST = lax.Precision.HIGHEST


def params(mebibytes):
    return pltpu.CompilerParams(vmem_limit_bytes=mebibytes * 1024 * 1024)


SMEM = pl.BlockSpec(memory_space=pltpu.SMEM)


def nn(a, b, precision=None):
    return lax.dot_general(
        a, b, (((1,), (0,)), ((), ())), precision=precision, preferred_element_type=F32
    )


def nt(a, b, precision=None):
    return lax.dot_general(
        a, b, (((1,), (1,)), ((), ())), precision=precision, preferred_element_type=F32
    )


def tn(a, b, precision=None):
    return lax.dot_general(
        a, b, (((0,), (0,)), ((), ())), precision=precision, preferred_element_type=F32
    )


def two_terms(value):
    high = value.astype(BF)
    return high, (value - high.astype(F32)).astype(BF)


def iota(shape, dim):
    return lax.broadcasted_iota(jnp.int32, shape, dim)


def turned(value, shift):
    width = value.shape[-1]
    tiles = [pltpu.roll(value[:, j : j + 128], shift, 1) for j in range(0, width, 128)]
    return jnp.concatenate(tiles, axis=1)


def norm_kernel(code_ref, turn_ref, tokens_ref, gain_ref, normed_ref, extra_ref):
    xf = tokens_ref[...].astype(F32)
    scale = lax.rsqrt(jnp.mean(xf * xf, axis=-1, keepdims=True) + EPS)
    normed = xf * scale * gain_ref[...].astype(F32)
    normed_ref[...] = turned(normed, (128 - turn_ref[0]) % 128).astype(BF)
    mean = jnp.mean(xf, axis=0, keepdims=True)
    rows = jnp.concatenate([mean[:, j * 128 : (j + 1) * 128] for j in range(8)], axis=0)
    high = rows.astype(BF).astype(F32)
    mid = (rows - high).astype(BF).astype(F32)
    low = rows - high - mid
    code = jnp.full((8, 128), code_ref[0], jnp.int32).astype(F32)
    extra_ref[:, :128] = jnp.concatenate([high, mid], axis=0).astype(BF)
    extra_ref[:, 128:] = jnp.concatenate([low, code], axis=0).astype(BF)


def gathered(refs):
    own, after, first, second, before = refs
    half = first.shape[0]
    rows = []
    for far in range(2 * half):
        across = first[far] if far < half else second[far - half]
        rows += [own[far], after[far], across, before[far]]
    return jnp.concatenate(rows, axis=0)


def grouped_rows(value):
    value = value.reshape(FRAMES, 2, 8, value.shape[-1])
    return jnp.concatenate([value[:, g].reshape(128, -1) for g in range(2)], axis=0)


def causal_same_patch():
    row, col = (iota((128, 128), 0), iota((128, 128), 1))
    return (row % 8 == col % 8) & (col // 8 <= row // 8)


def forward_heads(x_ref, weight_refs, qkv_ref, prob_ref):
    x = x_ref[...].reshape(256, D)
    for part in range(3):
        weight = gathered(weight_refs[part * PIECES : (part + 1) * PIECES])
        qkv_ref[part] = grouped_rows(nn(x, weight)).astype(BF)
    allowed = causal_same_patch()
    first = iota((128, 128), 1) < HEAD_DIM
    sums = []
    for pair in range(2):
        lanes = pl.ds(pair * 128, 128)
        total = jnp.zeros((FRAMES, 128), F32)
        for group in range(2):
            rows = pl.ds(group * 128, 128)
            q, k, v = (qkv_ref[part, rows, lanes] for part in range(3))
            mixed = []
            for j in range(2):
                own = jnp.where(first if j == 0 else ~first, q.astype(F32), 0.0).astype(BF)
                scores = jnp.where(allowed, nt(own, k) * HEAD_DIM ** (-0.5), -1e30)
                raised = jnp.exp(scores - jnp.max(scores, axis=1, keepdims=True))
                prob = raised * (1.0 / jnp.sum(raised, axis=1, keepdims=True))
                prob_ref[pair * 4 + group * 2 + j] = prob
                mixed.append(nn(prob.astype(BF), v))
            attended = jnp.where(first, mixed[0], mixed[1]).astype(BF).astype(F32)
            total = total + jnp.sum(attended.reshape(FRAMES, 8, 128), axis=1)
        sums.append(total)
    return jnp.concatenate(sums, axis=1)


def forward_own_kernel(x_ref, *refs):
    qkv_ref, prob_ref, sum_ref = refs[3 * PIECES :]
    sum_ref[...] = forward_heads(x_ref, refs[: 3 * PIECES], qkv_ref, prob_ref)


def forward_other_kernel(side_ref, x_ref, *refs):
    own_ref, extra_ref, qkv_ref, prob_ref, out_ref, sum_ref = refs[3 * PIECES :]
    step = pl.program_id(0)
    side = side_ref[0]

    @pl.when(step == 0)
    def _():
        sum_ref[:, pl.ds(pl.multiple_of(side * HALF, HALF), HALF)] = own_ref[...]

    at = pl.multiple_of((1 - side) * HALF + step * 256, 256)
    sum_ref[:, pl.ds(at, 256)] = forward_heads(x_ref, refs[: 3 * PIECES], qkv_ref, prob_ref)

    @pl.when(step == 1)
    def _():
        sums = sum_ref[...].astype(BF)
        for to in range(FRAMES):
            out_ref[to, :, :D] = sums
            out_ref[to, :, D:] = extra_ref[...]


def weight_specs(weight, at):
    return [
        pl.BlockSpec((*piece.shape[:2], 256), lambda i, part=part: (0, 0, part * 2 + at(i)))
        for part in range(3)
        for piece in weight
    ]


def whole(shape):
    return pl.BlockSpec(shape, lambda *_: (0,) * len(shape))


SAVED_SHAPES = (
    pltpu.HBM((3, 256, HALF), BF),
    pltpu.HBM((16, 128, 128), F32),
)


def saved_specs(at):
    return [
        pl.BlockSpec((3, 256, 256), lambda i: (0, 0, at(i))),
        pl.BlockSpec((8, 128, 128), lambda i: (at(i), 0, 0)),
    ]


def in_hbm(*values):
    return [pltpu.with_memory_space_constraint(v, pltpu.HBM) for v in values]


def forward_own(x, weight):
    return pl.pallas_call(
        forward_own_kernel,
        grid=(2,),
        in_specs=[whole((16, 16, D)), *weight_specs(weight, lambda i: i)],
        out_specs=[*saved_specs(lambda i: i), pl.BlockSpec((FRAMES, 256), lambda i: (0, i))],
        out_shape=(*SAVED_SHAPES, jax.ShapeDtypeStruct((FRAMES, HALF), F32)),
        compiler_params=params(16),
        name="forward_own",
    )(x, *weight * 3)


def forward_other(side, x, weight, own_sum, extra):
    return pl.pallas_call(
        forward_other_kernel,
        grid=(2,),
        in_specs=[
            SMEM,
            whole((16, 16, D)),
            *weight_specs(weight, lambda i: i),
            whole((FRAMES, HALF)),
            whole((16, EXTRA)),
        ],
        out_specs=[*saved_specs(lambda i: i), whole((16, 16, D + EXTRA))],
        out_shape=(*SAVED_SHAPES, pltpu.HBM((16, 16, D + EXTRA), BF)),
        scratch_shapes=[pltpu.VMEM((FRAMES, D), F32)],
        compiler_params=params(16),
        name="forward_other",
    )(side, x, *weight * 3, own_sum, extra)


def head_kernel(at_ref, got_ref, out_w_ref, pair_ref, book_ref, rows_ref, mean_ref, send_ref, pooled_ref):
    got = got_ref[...]
    sums = jnp.sum(got[:, :, :D].astype(F32), axis=0)
    first = got[:, :, D : D + 128].reshape(256, 128)
    second = got[:, :, D + 128 :].reshape(256, 128)
    row, col = (iota((128, 256), 0), iota((128, 256), 1))
    frame, piece = (row % 16, row // 16)
    same = col // 16 == frame
    pick_two = jnp.where(same & (col % 8 == piece), 1.0, 0.0).astype(BF)
    pick_one = jnp.where(same & (col % 16 == piece), 1.0, 0.0).astype(BF)
    means = nn(pick_two, first) + nn(pick_one, second)
    xmean = jnp.concatenate([means[j * 16 : (j + 1) * 16] for j in range(8)], axis=1)
    row, col = (iota((16, 256), 0), iota((16, 256), 1))
    pick_code = jnp.where(col == row * 16 + 8, 1.0, 0.0).astype(BF)
    code = nn(pick_code, second)
    out_w = out_w_ref[...]
    high, low = two_terms(sums)
    pooled = xmean + (nn(high, out_w) + nn(low, out_w)) / PATCHES
    now = nt(pooled, pair_ref[0], HIGHEST)
    later = nt(pooled, pair_ref[1], HIGHEST)
    zero = jnp.zeros((1, LATENT), F32)
    action = now + jnp.concatenate([later[1:], zero], axis=0)
    quantized = jnp.zeros((FRAMES, LATENT), F32)
    for k in range(CODES):
        quantized = quantized + jnp.where(code[:, :LATENT] == k, book_ref[k : k + 1, :], 0.0)
    d_action = 2.0 * BETA * (action - quantized)
    d_before = jnp.concatenate([zero, d_action[:-1]], axis=0)
    d_mean = nn(d_action, pair_ref[0], HIGHEST) + nn(d_before, pair_ref[1], HIGHEST)
    mean_ref[...] = d_mean
    high, low = two_terms(d_mean)
    rows_ref[...] = (nt(high, out_w) + nt(low, out_w)).astype(BF)
    pooled_ref[...] = pooled
    at = at_ref[0]
    block = pooled_ref[:, pl.ds(pl.multiple_of((at // 2) * 128, 128), 128)]
    own = jnp.where(at % 2 == 0, block, pltpu.roll(block, 64, 1))[:, :64]
    mine = jnp.concatenate([own, d_action, code[:, :LATENT]], axis=1)
    for to in range(send_ref.shape[0]):
        send_ref[to] = mine


def head(at, got, out_w, w_pair, codebook, clips):
    return pl.pallas_call(
        head_kernel,
        in_specs=[SMEM, *[pl.BlockSpec(memory_space=pltpu.VMEM)] * 4],
        out_shape=(
            pltpu.HBM((FRAMES, D), BF),
            pltpu.HBM((FRAMES, D), F32),
            pltpu.HBM((clips, FRAMES, 128), F32),
        ),
        scratch_shapes=[pltpu.VMEM((FRAMES, D), F32)],
        compiler_params=params(16),
        name="head",
    )(at, got, out_w, w_pair, codebook)


def backward_heads(rows_ref, at, qkv_ref, prob_ref, weight_refs, acc_ref):
    first = iota((128, 128), 1) < HEAD_DIM
    d_frames = rows_ref[:, pl.ds(at, 256)].astype(F32)
    d_all = jnp.broadcast_to(d_frames[:, None, :], (FRAMES, 8, 256)).reshape(128, 256)
    pieces = [[[None] * 2 for _ in range(2)] for _ in range(3)]
    for pair in range(2):
        lanes = pl.ds(pair * 128, 128)
        d_wide = d_all[:, pair * 128 : (pair + 1) * 128]
        d_out = d_wide.astype(BF)
        for group in range(2):
            rows = pl.ds(group * 128, 128)
            q, k, v = (qkv_ref[part, rows, lanes] for part in range(3))
            found = []
            for j in range(2):
                prob = prob_ref[pair * 4 + group * 2 + j]
                own = jnp.where(first if j == 0 else ~first, d_wide, 0.0).astype(BF)
                d_weights = nt(own, v).astype(BF).astype(F32)
                inner = jnp.sum(d_weights * prob, axis=1, keepdims=True)
                d_scores = (prob * (d_weights - inner) * HEAD_DIM ** (-0.5)).astype(BF)
                found.append((nn(d_scores, k), tn(d_scores, q), tn(prob.astype(BF), d_out)))
            for part in range(3):
                pieces[part][pair][group] = jnp.where(first, found[0][part], found[1][part]).astype(BF)
    total = None
    for part in range(3):
        d_part = jnp.concatenate(
            [jnp.concatenate(pieces[part][pair], axis=0) for pair in range(2)], axis=1
        )
        term = nt(d_part, gathered(weight_refs[part * PIECES : (part + 1) * PIECES]))
        total = term if total is None else total + term
    acc_ref[...] += total


def backward_kernel(side_ref, rows_ref, *refs):
    each = 2 + 3 * PIECES
    own, other = (refs[:each], refs[each : 2 * each])
    out_ref, acc_ref = refs[2 * each :]
    step = pl.program_id(0)
    side = side_ref[0]

    @pl.when(step == 0)
    def _():
        acc_ref[...] = jnp.zeros_like(acc_ref)

    @pl.when(step < 2)
    def _():
        at = pl.multiple_of(side * HALF + step * 256, 256)
        backward_heads(rows_ref, at, own[0], own[1], own[2:], acc_ref)

    @pl.when(step >= 2)
    def _():
        at = pl.multiple_of((1 - side) * HALF + (step - 2) * 256, 256)
        backward_heads(rows_ref, at, other[0], other[1], other[2:], acc_ref)

    @pl.when(step == 3)
    def _():
        acc = acc_ref[...].reshape(2, FRAMES, 8, D)
        both = jnp.concatenate([acc[0][:, None], acc[1][:, None]], axis=1)
        out_ref[...] = both.reshape(FRAMES, 16, D).astype(BF)


def backward(side, d_rows, own, other):
    def early(i):
        return jnp.minimum(i, 1)

    def late(i):
        return jnp.maximum(i - 2, 0)

    return pl.pallas_call(
        backward_kernel,
        grid=(4,),
        in_specs=[
            SMEM,
            whole((FRAMES, D)),
            *saved_specs(early),
            *weight_specs(own[2], early),
            *saved_specs(late),
            *weight_specs(other[2], late),
        ],
        out_specs=whole((16, 16, D)),
        out_shape=pltpu.HBM((16, 16, D + GRADS), BF),
        scratch_shapes=[pltpu.VMEM((256, D), F32)],
        compiler_params=params(24),
        name="backward",
    )(side, d_rows, *in_hbm(*own[:2]), *own[2] * 3, *in_hbm(*other[:2]), *other[2] * 3)


def grads_kernel(_, got_ref, out_ref, step_ref):
    count = got_ref.shape[0] * FRAMES
    got = got_ref[...].reshape(count, 128)
    frame = iota((count, 128), 0) % FRAMES
    before = jnp.where(frame == 0, 0.0, pltpu.roll(got, 1, 0))
    onehot = jnp.where(got[:, 96:97] == iota((count, 128), 1).astype(F32), 1.0, 0.0)
    onehot = jnp.where(iota((count, 128), 1) < CODES, onehot, 0.0)
    now = tn(got, got, HIGHEST)[64:96]
    later = tn(before, got, HIGHEST)[64:96]
    both = jnp.concatenate([now, later], axis=0)
    high = both.astype(BF).astype(F32)
    low = both - high
    packed = jnp.where(iota((64, 128), 1) < 64, high, pltpu.roll(low, 64, 1)).astype(BF)
    for to in range(FRAMES):
        for q in range(4):
            out_ref[to, :, q * 128 : (q + 1) * 128] = packed[q * 16 : (q + 1) * 16]
    by_code = tn(onehot, got, HIGHEST)[:CODES, 64:96] * (-1.0 / BETA)
    counted = tn(onehot, jnp.ones((count, 128), F32), HIGHEST)[:CODES, :LATENT]
    step_ref[...] = by_code / counted


def grads(partly, got):
    return pl.pallas_call(
        grads_kernel,
        grid=(1,),
        in_specs=[pl.BlockSpec(memory_space=pl.ANY), whole(got.shape)],
        out_specs=[
            pl.BlockSpec((16, 16, GRADS), lambda i: (0, 0, D // GRADS)),
            whole((CODES, LATENT)),
        ],
        out_shape=(
            pltpu.HBM(partly.shape, BF),
            jax.ShapeDtypeStruct((CODES, LATENT), F32),
        ),
        input_output_aliases={0: 0},
        compiler_params=params(8),
        name="grads",
    )(*in_hbm(partly), got)


def last_kernel(at_ref, turn_ref, got_ref, tokens_ref, gain_ref, mean_ref, out_ref, pair_ref):
    xf = tokens_ref[...].astype(F32)
    scale = lax.rsqrt(jnp.mean(xf * xf, axis=-1, keepdims=True) + EPS)
    d_normed = turned(got_ref[:, :, :D].reshape(xf.shape).astype(F32), turn_ref[0])
    d_scaled = d_normed * gain_ref[...].astype(F32)
    inner = jnp.sum(d_scaled * xf, axis=-1, keepdims=True) / D
    d_through = d_scaled * scale - xf * (scale * scale * scale * inner)
    d_resid = mean_ref[pl.ds(at_ref[0], 1), :]
    out_ref[...] = (d_resid + d_through).astype(BF)
    even = iota((16, 128), 1) < 64
    for t in range(0, 4, 2):
        for q in range(4):
            terms = [got_ref[t + n, :, D + q * 128 : D + (q + 1) * 128].astype(F32) for n in range(2)]
            value = [term + pltpu.roll(term, 64, 1) for term in terms]
            rows, lanes = (pl.ds(q % 2 * 16, 16), pl.ds(t * 64, 128))
            pair_ref[q // 2, rows, lanes] = jnp.where(even, value[0], value[1])


def last(at, turn, got, tokens, gain, d_mean):
    return pl.pallas_call(
        last_kernel,
        grid=(4,),
        in_specs=[
            SMEM,
            SMEM,
            pl.BlockSpec((4, 16, D + GRADS), lambda i: (i, 0, 0)),
            pl.BlockSpec((64, D), lambda i: (i, 0)),
            whole((1, D)),
            whole((FRAMES, D)),
        ],
        out_specs=[
            pl.BlockSpec((64, D), lambda i: (i, 0)),
            pl.BlockSpec((2, LATENT, 256), lambda i: (0, 0, i)),
        ],
        out_shape=(
            jax.ShapeDtypeStruct((PATCHES, D), BF),
            jax.ShapeDtypeStruct((2, LATENT, D), F32),
        ),
        compiler_params=params(8),
        name="last",
    )(at, turn, got, tokens, gain, d_mean)


def sent_to_all(value, axis):
    count = lax.axis_size(axis)
    return lax.all_to_all(
        jnp.broadcast_to(value[None], (count, *value.shape)), axis, 0, 0, tiled=True
    )


def shifted(value, axis, by):
    count = lax.axis_size(axis)
    return lax.ppermute(value, axis, [(i, (i + by) % count) for i in range(count)])


def local(tokens, gain, w_qkv, w_out, w_pair, codebook, codes):
    side = lax.axis_index("tm_1")
    at = lax.axis_index(TM).reshape(1)
    turn = (lax.axis_index("dp_1") * 32).reshape(1)
    rows = w_qkv.shape[0]
    tokens = tokens.reshape(PATCHES, D)
    gain = gain.reshape(1, D)
    full_out = lax.all_gather(w_out, DP, axis=0, tiled=True)
    by_side = [
        jnp.concatenate([w_qkv[:, p * D + s * HALF :][:, :HALF] for p in range(3)], axis=1)
        for s in range(2)
    ]
    near = sent_to_all(jnp.where(side == 0, *by_side), "dp_0")
    half = near.shape[0] // 2
    after = shifted(near, "dp_1", -1)
    before = shifted(near, "dp_1", 1)
    first = shifted(before[:half], "dp_1", 1)
    second = shifted(after[half:], "dp_1", -1)
    own_w = [near, after, first, second, before]
    other_w = [shifted(piece, "tm_1", 1) for piece in own_w]
    side = side.reshape(1)

    normed, extra = pl.pallas_call(
        norm_kernel,
        in_specs=[SMEM, SMEM, *[pl.BlockSpec(memory_space=pltpu.VMEM)] * 2],
        out_shape=(
            jax.ShapeDtypeStruct((PATCHES, D), BF),
            jax.ShapeDtypeStruct((16, EXTRA), BF),
        ),
        compiler_params=params(8),
        name="norm",
    )(codes.reshape(1), turn, tokens, gain)
    x = lax.all_to_all(normed.reshape(16, 16, D), TM, 0, 0, tiled=True)

    own_qkv, own_prob, own_sum = forward_own(x, own_w)
    other_qkv, other_prob, partial = forward_other(side, x, other_w, own_sum, extra)
    arrived = lax.all_to_all(partial, TM, 0, 0, tiled=True)
    clips = lax.axis_size(DP)
    pair = jnp.swapaxes(w_pair, 1, 2)
    d_rows, d_mean, mine = head(at, arrived, full_out, pair, codebook, clips)
    everyone = lax.all_to_all(mine, DP, 0, 0, tiled=True)
    partly = backward(
        side, d_rows, (own_qkv, own_prob, own_w), (other_qkv, other_prob, other_w)
    )
    outgoing, codebook_step = grads(partly, everyone)
    back = lax.all_to_all(outgoing, TM, 0, 0, tiled=True)
    grad_tokens, grad_pair = last(at, turn, back, tokens, gain, d_mean)
    return (
        grad_tokens.reshape(1, 1, PATCHES, D),
        jnp.swapaxes(grad_pair, 1, 2),
        codebook_step,
    )


def solution(mesh):
    torus = Mesh(mesh.devices.reshape(8, 4, 8, 2), ("dp_0", "dp_1", "tm_0", "tm_1"))
    return jax.shard_map(
        local,
        mesh=torus,
        in_specs=(P(DP, TM, None, None), P(), P(DP, None), P(DP, None), P(), P(), P(DP, TM, None)),
        out_specs=(P(DP, TM, None, None), P(), P()),
        check_vma=False,
    )
```

```python
import jax
import jax.numpy as jnp
from jax import lax
from jax.experimental import pallas as pl
from jax.experimental.pallas import tpu as pltpu
from jax.sharding import Mesh
from jax.sharding import PartitionSpec as P

D = 1024
HEAD_DIM = 64
LATENT = 32
CODES = 8
PATCHES = 256
FRAMES = 16
EPS = 1e-06
BETA = 0.25
DP = ("dp_0", "dp_1")
TM = ("tm_0", "tm_1")
HALF = 512
EXTRA = 256
GRADS = 256
PIECES = 5
GROUPS = 4
ROWS = 512
BF = jnp.bfloat16
F32 = jnp.float32
HIGHEST = lax.Precision.HIGHEST


def params(mebibytes):
    return pltpu.CompilerParams(vmem_limit_bytes=mebibytes * 1024 * 1024)


SMEM = pl.BlockSpec(memory_space=pltpu.SMEM)


def nn(a, b, precision=None):
    return lax.dot_general(
        a, b, (((1,), (0,)), ((), ())), precision=precision, preferred_element_type=F32
    )


def nt(a, b, precision=None):
    return lax.dot_general(
        a, b, (((1,), (1,)), ((), ())), precision=precision, preferred_element_type=F32
    )


def tn(a, b, precision=None):
    return lax.dot_general(
        a, b, (((0,), (0,)), ((), ())), precision=precision, preferred_element_type=F32
    )


def two_terms(value):
    high = value.astype(BF)
    return high, (value - high.astype(F32)).astype(BF)


def iota(shape, dim):
    return lax.broadcasted_iota(jnp.int32, shape, dim)


def turned(value, shift):
    width = value.shape[-1]
    tiles = [pltpu.roll(value[:, j : j + 128], shift, 1) for j in range(0, width, 128)]
    return jnp.concatenate(tiles, axis=1)


def share_kernel(side_ref, weight_ref, out_ref):
    for part in range(3):
        at = pl.multiple_of(part * D + side_ref[0] * HALF, HALF)
        value = weight_ref[:, pl.ds(at, HALF)]
        for to in range(out_ref.shape[0]):
            out_ref[to, :, part * HALF : (part + 1) * HALF] = value


def share(side, weight, count):
    return pl.pallas_call(
        share_kernel,
        in_specs=[SMEM, pl.BlockSpec(memory_space=pltpu.VMEM)],
        out_shape=jax.ShapeDtypeStruct((count, weight.shape[0], 3 * HALF), BF),
        compiler_params=params(8),
        name="share",
    )(side, weight)


def norm_kernel(code_ref, turn_ref, tokens_ref, gain_ref, _, normed_ref, extra_ref):
    xf = tokens_ref[...].astype(F32)
    scale = lax.rsqrt(jnp.mean(xf * xf, axis=-1, keepdims=True) + EPS)
    normed = xf * scale * gain_ref[...].astype(F32)
    normed_ref[...] = turned(normed, (128 - turn_ref[0]) % 128).astype(BF)
    mean = jnp.mean(xf, axis=0, keepdims=True)
    rows = jnp.concatenate([mean[:, j * 128 : (j + 1) * 128] for j in range(8)], axis=0)
    high = rows.astype(BF).astype(F32)
    mid = (rows - high).astype(BF).astype(F32)
    low = rows - high - mid
    code = jnp.full((8, 128), code_ref[0], jnp.int32).astype(F32)
    extra_ref[:, :128] = jnp.concatenate([high, mid], axis=0).astype(BF)
    extra_ref[:, 128:] = jnp.concatenate([low, code], axis=0).astype(BF)


def gathered(refs):
    own, after, first, second, before = refs
    half = first.shape[0]
    rows = []
    for far in range(2 * half):
        across = first[far] if far < half else second[far - half]
        rows += [own[far], after[far], across, before[far]]
    return jnp.concatenate(rows, axis=0)


def grouped_rows(value):
    value = value.reshape(FRAMES, GROUPS, 8, value.shape[-1])
    return jnp.concatenate([value[:, g].reshape(128, -1) for g in range(GROUPS)], axis=0)


def frame_of(row):
    return row % 8 * 2 + row // 8


def causal_same_patch():
    row, col = (iota((128, 128), 0), iota((128, 128), 1))
    return (row % 8 == col % 8) & (frame_of(col // 8) <= frame_of(row // 8))


def head_masks():
    lane = iota((1, 128), 1)
    return tuple(jnp.where(lane // HEAD_DIM == j, 1.0, 0.0).astype(BF) for j in range(2))


def by_head(value, masks):
    return jnp.concatenate([value * mask for mask in masks], axis=0)


def units():
    return [(pair, group, pair * GROUPS + group) for pair in range(2) for group in range(GROUPS)]


def forward_heads(x_ref, weight_refs, qkv_ref, prob_ref):
    x = x_ref[...].reshape(ROWS, D)
    for part in range(3):
        weight = gathered(weight_refs[part * PIECES : (part + 1) * PIECES])
        qkv_ref[part] = grouped_rows(nn(x, weight)).astype(BF)
    allowed = causal_same_patch()
    masks = head_masks()

    def taken(part, pair, group):
        return qkv_ref[part, pl.ds(group * 128, 128), pl.ds(pair * 128, 128)]

    for pair, group, unit in units():
        scores = nt(by_head(taken(0, pair, group), masks), taken(1, pair, group))
        for j in range(2):
            one = scores[j * 128 : (j + 1) * 128] * HEAD_DIM ** (-0.5)
            prob_ref[unit * 2 + j] = jnp.where(allowed, one, -1e30)
    for at in range(16):
        scores = prob_ref[at]
        raised = jnp.exp(scores - jnp.max(scores, axis=1, keepdims=True))
        prob_ref[at] = raised * (1.0 / jnp.sum(raised, axis=1, keepdims=True))
    totals = [jnp.zeros((FRAMES, 128), F32)] * 2
    for pair, group, unit in units():
        weights = jnp.concatenate([prob_ref[unit * 2 + j] for j in range(2)], axis=1).astype(BF)
        mixed = nn(weights, by_head(taken(2, pair, group), masks))
        attended = mixed.astype(BF).astype(F32)
        totals[pair] = totals[pair] + jnp.sum(attended.reshape(FRAMES, 8, 128), axis=1)
    return jnp.concatenate(totals, axis=1)


def forward_kernel(_, side_ref, same_ref, cross_ref, *refs):
    extra_ref, qkv_ref, prob_ref, out_ref, x_ref, sum_ref = refs[3 * PIECES :]
    step = pl.program_id(0)

    @pl.when(step == 0)
    def _():
        x_ref[side_ref[0]] = same_ref[...]
        x_ref[1 - side_ref[0]] = cross_ref[...]

    lanes = pl.ds(pl.multiple_of(step * 256, 256), 256)
    sum_ref[:, lanes] = forward_heads(x_ref, refs[: 3 * PIECES], qkv_ref, prob_ref)

    @pl.when(step == 1)
    def _():
        sums = sum_ref[...].astype(BF)
        for to in range(FRAMES):
            out_ref[to, :, :HALF] = sums
            out_ref[to, :, HALF:] = extra_ref[...]


def weight_specs(weight):
    return [
        pl.BlockSpec((*piece.shape[:2], 256), lambda i, part=part: (0, 0, part * 2 + i))
        for part in range(3)
        for piece in weight
    ]


def whole(shape):
    return pl.BlockSpec(shape, lambda *_: (0,) * len(shape))


SAVED_SHAPES = (
    pltpu.HBM((3, ROWS, HALF), BF),
    pltpu.HBM((32, 128, 128), F32),
)


def saved_specs():
    return [
        pl.BlockSpec((3, ROWS, 256), lambda i: (0, 0, i)),
        pl.BlockSpec((16, 128, 128), lambda i: (i, 0, 0)),
    ]


def in_hbm(*values):
    return [pltpu.with_memory_space_constraint(v, pltpu.HBM) for v in values]


def forward(ready, side, same, cross, weight, extra):
    return pl.pallas_call(
        forward_kernel,
        grid=(2,),
        in_specs=[
            pl.BlockSpec(memory_space=pl.ANY),
            SMEM,
            whole(same.shape),
            whole(cross.shape),
            *weight_specs(weight),
            whole((16, EXTRA)),
        ],
        out_specs=[*saved_specs(), whole((16, 16, HALF + EXTRA))],
        out_shape=(*SAVED_SHAPES, pltpu.HBM((16, 16, HALF + EXTRA), BF)),
        scratch_shapes=[pltpu.VMEM((2, 8, 32, D), BF), pltpu.VMEM((FRAMES, HALF), F32)],
        compiler_params=params(24),
        cost_estimate=cost(1_000),
        name="forward",
    )(ready, side, same, cross, *weight * 3, extra)


def head_kernel(
    at_ref, got_ref, out_w_hbm, pair_hbm, book_ref, rows_ref, mean_ref, send_ref, *scratch
):
    pooled_ref, out_w_ref, pair_ref, sem = scratch
    copies = [
        pltpu.make_async_copy(out_w_hbm, out_w_ref, sem.at[0]),
        pltpu.make_async_copy(pair_hbm, pair_ref, sem.at[1]),
    ]
    for copy in copies:
        copy.start()
    got = got_ref[...].reshape(8, 2, 16, HALF + EXTRA)
    sums = [jnp.sum(got[:, c, :, :HALF].astype(F32), axis=0) for c in range(2)]
    sums = jnp.concatenate(sums, axis=1)
    got = got.reshape(16, 16, HALF + EXTRA)
    first = got[:, :, HALF : HALF + 128].reshape(256, 128)
    second = got[:, :, HALF + 128 :].reshape(256, 128)
    row, col = (iota((128, 256), 0), iota((128, 256), 1))
    frame, piece = (frame_of(row % 16), row // 16)
    same = col // 16 == frame
    pick_two = jnp.where(same & (col % 8 == piece), 1.0, 0.0).astype(BF)
    pick_one = jnp.where(same & (col % 16 == piece), 1.0, 0.0).astype(BF)
    means = nn(pick_two, first) + nn(pick_one, second)
    xmean = jnp.concatenate([means[j * 16 : (j + 1) * 16] for j in range(8)], axis=1)
    row, col = (iota((16, 256), 0), iota((16, 256), 1))
    pick_code = jnp.where(col == frame_of(row) * 16 + 8, 1.0, 0.0).astype(BF)
    code = nn(pick_code, second)
    for copy in copies:
        copy.wait()
    sums = jnp.concatenate(two_terms(sums), axis=0)
    moved = nn(sums, out_w_ref[...])
    pooled = xmean + (moved[:FRAMES] + moved[FRAMES:]) / PATCHES
    now = nt(pooled, pair_ref[0], HIGHEST)
    later = nt(pooled, pair_ref[1], HIGHEST)
    zero = jnp.zeros((1, LATENT), F32)
    action = now + jnp.concatenate([later[8:], later[1:8], zero], axis=0)
    quantized = jnp.zeros((FRAMES, LATENT), F32)
    for k in range(CODES):
        quantized = quantized + jnp.where(code[:, :LATENT] == k, book_ref[k : k + 1, :], 0.0)
    d_action = 2.0 * BETA * (action - quantized)
    d_before = jnp.concatenate([zero, d_action[8:15], d_action[:8]], axis=0)
    d_mean = nn(d_action, pair_ref[0], HIGHEST) + nn(d_before, pair_ref[1], HIGHEST)
    mean_ref[...] = d_mean
    terms = jnp.concatenate(two_terms(d_mean), axis=0)
    both = nt(terms, out_w_ref[...])
    rows_ref[...] = (both[:FRAMES] + both[FRAMES:]).astype(BF)
    pooled_ref[...] = pooled
    mine = pooled_ref[:, pl.ds(pl.multiple_of(at_ref[0] * 128, 128), 128)]
    high, low = two_terms(d_action)
    others = [mine.astype(BF), high, low, code[:, : 2 * LATENT].astype(BF)]
    mine = jnp.concatenate(others, axis=1)
    for to in range(send_ref.shape[0]):
        send_ref[to] = mine


def head(at, got, out_w, w_pair, codebook, clips):
    return pl.pallas_call(
        head_kernel,
        in_specs=[
            SMEM,
            pl.BlockSpec(memory_space=pltpu.VMEM),
            *[pl.BlockSpec(memory_space=pl.ANY)] * 2,
            pl.BlockSpec(memory_space=pltpu.VMEM),
        ],
        out_shape=(
            pltpu.HBM((FRAMES, D), BF),
            pltpu.HBM((FRAMES, D), F32),
            pltpu.HBM((clips, FRAMES, 256), BF),
        ),
        scratch_shapes=[
            pltpu.VMEM((FRAMES, D), F32),
            pltpu.VMEM((D, D), BF),
            pltpu.VMEM((2, LATENT, D), F32),
            pltpu.SemaphoreType.DMA((2,)),
        ],
        compiler_params=params(16),
        cost_estimate=cost(1_000),
        name="head",
    )(at, got, *in_hbm(out_w, w_pair), codebook)


def backward_heads(rows_ref, at, qkv_ref, prob_ref, weight_refs, acc_ref, cot_ref, part_ref):
    masks = head_masks()
    d_frames = rows_ref[:, pl.ds(at, 256)].astype(F32)
    d_all = jnp.broadcast_to(d_frames[:, None, :], (FRAMES, 8, 256)).reshape(128, 256).astype(BF)
    d_heads = [by_head(d_all[:, pair * 128 : (pair + 1) * 128], masks) for pair in range(2)]

    def taken(part, pair, group):
        return qkv_ref[part, pl.ds(group * 128, 128), pl.ds(pair * 128, 128)]

    for pair, group, unit in units():
        d_weights = nt(d_heads[pair], taken(2, pair, group))
        for j in range(2):
            cot_ref[unit * 2 + j] = d_weights[j * 128 : (j + 1) * 128].astype(BF)
    for index in range(16):
        prob = prob_ref[index]
        d_weights = cot_ref[index].astype(F32)
        inner = jnp.sum(d_weights * prob, axis=1, keepdims=True)
        cot_ref[index] = (prob * (d_weights - inner) * HEAD_DIM ** (-0.5)).astype(BF)
    for pair, group, unit in units():
        d_scores = [cot_ref[unit * 2 + j] for j in range(2)]
        prob = jnp.concatenate([prob_ref[unit * 2 + j].astype(BF) for j in range(2)], axis=0)
        d_query = nn(jnp.concatenate(d_scores, axis=1), by_head(taken(1, pair, group), masks))
        d_keys = tn(jnp.concatenate(d_scores, axis=0), by_head(taken(0, pair, group), masks))
        d_values = tn(prob, d_heads[pair])
        for part, value in enumerate((d_query, d_keys, d_values)):
            part_ref[part, pl.ds(group * 128, 128), pl.ds(pair * 128, 128)] = value.astype(BF)
    total = None
    for part in range(3):
        term = nt(part_ref[part], gathered(weight_refs[part * PIECES : (part + 1) * PIECES]))
        total = term if total is None else total + term
    acc_ref[...] += total


def backward_kernel(side_ref, rows_ref, *refs):
    keep_ref, give_ref, acc_ref, parts_ref, *scratch = refs[2 + 3 * PIECES :]
    step = pl.program_id(0)
    side = side_ref[0]

    @pl.when(step == 0)
    def _():
        acc_ref[...] = jnp.zeros_like(acc_ref)

    at = pl.multiple_of(side * HALF + step * 256, 256)
    backward_heads(rows_ref, at, refs[0], refs[1], refs[2 : 2 + 3 * PIECES], acc_ref, *scratch)

    @pl.when(step == 1)
    def _():
        for group in range(GROUPS):
            rows = acc_ref[pl.ds(group * 128, 128), :].reshape(2, 8, 8, D)
            parts_ref[:, :, pl.ds(group * 8, 8), :] = rows
        keep_ref[...] = parts_ref[side]
        give_ref[...] = parts_ref[1 - side].astype(BF)


def backward(side, d_rows, qkv, prob, weight):
    return pl.pallas_call(
        backward_kernel,
        grid=(2,),
        in_specs=[SMEM, whole((FRAMES, D)), *saved_specs(), *weight_specs(weight)],
        out_specs=[whole((8, 32, D))] * 2,
        out_shape=(pltpu.HBM((8, 32, D), F32), jax.ShapeDtypeStruct((8, 32, D), BF)),
        scratch_shapes=[
            pltpu.VMEM((ROWS, D), F32),
            pltpu.VMEM((2, 8, 32, D), F32),
            pltpu.VMEM((16, 128, 128), BF),
            pltpu.VMEM((3, ROWS, 256), BF),
        ],
        compiler_params=params(32),
        cost_estimate=cost(1_000),
        name="backward",
    )(side, *in_hbm(d_rows, qkv, prob), *weight * 3)


def grads_kernel(_, keep_ref, cross_ref, got_ref, out_ref, step_ref):
    count = got_ref.shape[0] * FRAMES
    got = got_ref[...].reshape(count, 256)
    means, others = (got[:, :128], got[:, 128:])
    wide = others.astype(F32)
    place, lane = (iota((count, 128), 0) % FRAMES, iota((count, 128), 1))
    shift = jnp.where(place == 0, 0.0, pltpu.roll(wide, count - 7, 0))
    before = jnp.where(place >= 8, pltpu.roll(wide, 8, 0), shift).astype(BF)
    code = wide[:, 2 * LATENT : 2 * LATENT + 1]
    onehot = jnp.where((code == lane.astype(F32)) & (lane < CODES), 1.0, 0.0).astype(BF)
    for part, value in enumerate((others, before)):
        terms = tn(value, means)
        total = (terms[:LATENT] + terms[LATENT : 2 * LATENT]).astype(BF)
        for to in range(8):
            out_ref[to, :, D + part * 128 : D + (part + 1) * 128] = total
    counted = jnp.where(lane < 2 * LATENT, wide, 1.0).astype(BF)
    totals = tn(onehot, counted)[:CODES]
    by_code = (totals[:, :LATENT] + totals[:, LATENT : 2 * LATENT]) * (-1.0 / BETA)
    out_ref[:, :, :D] = (keep_ref[...] + cross_ref[...].astype(F32)).astype(BF)
    step_ref[...] = by_code / totals[:, 2 * LATENT : 2 * LATENT + 1]


def grads(ready, keep, cross, got):
    return pl.pallas_call(
        grads_kernel,
        in_specs=[pl.BlockSpec(memory_space=pl.ANY), *[pl.BlockSpec(memory_space=pltpu.VMEM)] * 3],
        out_shape=(
            pltpu.HBM((8, 32, D + GRADS), BF),
            jax.ShapeDtypeStruct((CODES, LATENT), F32),
        ),
        compiler_params=params(8),
        cost_estimate=cost(1_000),
        name="grads",
    )(ready, keep, cross, got)


def last_kernel(at_ref, turn_ref, got_ref, tokens_ref, gain_ref, mean_ref, out_ref, pair_ref):
    xf = tokens_ref[...].astype(F32)
    scale = lax.rsqrt(jnp.mean(xf * xf, axis=-1, keepdims=True) + EPS)
    d_normed = turned(got_ref[:, :, :D].reshape(xf.shape).astype(F32), turn_ref[0])
    d_scaled = d_normed * gain_ref[...].astype(F32)
    inner = jnp.sum(d_scaled * xf, axis=-1, keepdims=True) / D
    d_through = d_scaled * scale - xf * (scale * scale * scale * inner)
    d_resid = mean_ref[pl.ds(at_ref[0], 1), :]
    out_ref[...] = (d_resid + d_through).astype(BF)
    for t in range(2):
        for part in range(2):
            value = got_ref[t, :, pl.ds(D + part * 128, 128)]
            pair_ref[part, :, pl.ds(t * 128, 128)] = value.astype(F32)


def last(at, turn, got, tokens, gain, d_mean):
    return pl.pallas_call(
        last_kernel,
        grid=(4,),
        in_specs=[
            SMEM,
            SMEM,
            pl.BlockSpec((2, 32, D + GRADS), lambda i: (i, 0, 0)),
            pl.BlockSpec((64, D), lambda i: (i, 0)),
            whole((1, D)),
            whole((FRAMES, D)),
        ],
        out_specs=[
            pl.BlockSpec((64, D), lambda i: (i, 0)),
            pl.BlockSpec((2, LATENT, 256), lambda i: (0, 0, i)),
        ],
        out_shape=(
            jax.ShapeDtypeStruct((PATCHES, D), BF),
            jax.ShapeDtypeStruct((2, LATENT, D), F32),
        ),
        compiler_params=params(8),
        name="last",
    )(at, turn, got, tokens, gain, d_mean)


def cost(flops):
    return pl.CostEstimate(flops=flops, transcendentals=0, bytes_accessed=0)


def touch_kernel(*refs):
    refs[-1][...] = jnp.zeros_like(refs[-1])


def touched(flops, *values):
    return pl.pallas_call(
        touch_kernel,
        in_specs=[pl.BlockSpec(memory_space=pltpu.VMEM)] * len(values),
        out_shape=pltpu.HBM((8, 128), F32),
        compiler_params=params(4),
        cost_estimate=cost(flops),
        name="touch",
    )(*values)


def shifted(value, axis, by):
    count = lax.axis_size(axis)
    return lax.ppermute(value, axis, [(i, (i + by) % count) for i in range(count)])


def local(tokens, gain, w_qkv, w_out, w_pair, codebook, codes):
    side = lax.axis_index("tm_1")
    layer = lax.axis_index("tm_0")
    turn = (lax.axis_index("dp_1") * 32).reshape(1)
    rows = w_qkv.shape[0]
    tokens = tokens.reshape(PATCHES, D)
    gain = gain.reshape(1, D)
    full_out = lax.all_gather(w_out, DP, axis=0, tiled=True)
    far = lax.axis_size("dp_0")
    near = lax.all_to_all(share(side.reshape(1), w_qkv, far), "dp_0", 0, 0, tiled=True)
    half = near.shape[0] // 2
    after = shifted(near, "dp_1", -1)
    before = shifted(near, "dp_1", 1)
    first = shifted(before[:half], "dp_1", 1)
    second = shifted(after[half:], "dp_1", -1)
    own_w = [near, after, first, second, before]
    at = (side * 8 + layer).reshape(1)
    layer = layer.reshape(1)
    side = side.reshape(1)

    normed, extra = pl.pallas_call(
        norm_kernel,
        in_specs=[
            SMEM,
            SMEM,
            *[pl.BlockSpec(memory_space=pltpu.VMEM)] * 2,
            pl.BlockSpec(memory_space=pl.ANY),
        ],
        out_shape=(
            pltpu.HBM((PATCHES, D), BF),
            jax.ShapeDtypeStruct((16, EXTRA), BF),
        ),
        compiler_params=params(8),
        cost_estimate=cost(1_000),
        name="norm",
    )(codes.reshape(1), turn, tokens, gain, near)
    same = lax.all_to_all(normed.reshape(8, 32, D), "tm_0", 0, 0, tiled=True)
    cross = shifted(same, "tm_1", 1)
    qkv, prob, partial = forward(touched(10_000_000_000, first, second), side, same, cross, own_w, extra)
    arrived = lax.all_to_all(partial, TM, 0, 0, tiled=True)
    clips = lax.axis_size(DP)
    pair = jnp.swapaxes(w_pair, 1, 2)
    d_rows, d_mean, mine = head(layer, arrived, full_out, pair, codebook, clips)
    everyone = lax.all_to_all(mine, DP, 0, 0, tiled=True)
    keep, give = backward(side, d_rows, qkv, prob, own_w)
    ready = touched(1_000_000_000, everyone)
    outgoing, codebook_step = grads(ready, keep, shifted(give, "tm_1", 1), everyone)
    back = lax.all_to_all(outgoing, "tm_0", 0, 0, tiled=True)
    grad_tokens, grad_pair = last(at, turn, back, tokens, gain, d_mean)
    return (
        grad_tokens.reshape(1, 1, PATCHES, D),
        jnp.swapaxes(grad_pair, 1, 2),
        codebook_step,
    )


def solution(mesh):
    torus = Mesh(mesh.devices.reshape(8, 4, 8, 2), ("dp_0", "dp_1", "tm_0", "tm_1"))
    return jax.shard_map(
        local,
        mesh=torus,
        in_specs=(P(DP, TM, None, None), P(), P(DP, None), P(DP, None), P(), P(), P(DP, TM, None)),
        out_specs=(P(DP, TM, None, None), P(), P()),
        check_vma=False,
    )
```

```python
import jax
import jax.numpy as jnp
from jax import lax
from jax.experimental import pallas as pl
from jax.experimental.pallas import tpu as pltpu
from jax.sharding import Mesh
from jax.sharding import PartitionSpec as P

D = 1024
HEAD_DIM = 64
LATENT = 32
CODES = 8
PATCHES = 256
FRAMES = 16
EPS = 1e-06
BETA = 0.25
DP = ("dp_0", "dp_1")
TM = ("tm_0", "tm_1")
HALF = 512
EXTRA = 256
GRADS = 256
PIECES = 7
GROUPS = 4
ROWS = 512
BF = jnp.bfloat16
F32 = jnp.float32
HIGHEST = lax.Precision.HIGHEST


def params(mebibytes):
    return pltpu.CompilerParams(vmem_limit_bytes=mebibytes * 1024 * 1024)


SMEM = pl.BlockSpec(memory_space=pltpu.SMEM)


def nn(a, b, precision=None):
    return lax.dot_general(
        a, b, (((1,), (0,)), ((), ())), precision=precision, preferred_element_type=F32
    )


def nt(a, b, precision=None):
    return lax.dot_general(
        a, b, (((1,), (1,)), ((), ())), precision=precision, preferred_element_type=F32
    )


def tn(a, b, precision=None):
    return lax.dot_general(
        a, b, (((0,), (0,)), ((), ())), precision=precision, preferred_element_type=F32
    )


def two_terms(value):
    high = value.astype(BF)
    return high, (value - high.astype(F32)).astype(BF)


def iota(shape, dim):
    return lax.broadcasted_iota(jnp.int32, shape, dim)


def turned(value, shift):
    width = value.shape[-1]
    tiles = [pltpu.roll(value[:, j : j + 128], shift, 1) for j in range(0, width, 128)]
    return jnp.concatenate(tiles, axis=1)


def share_kernel(side_ref, weight_ref, out_ref):
    for part in range(3):
        at = pl.multiple_of(part * D + side_ref[0] * HALF, HALF)
        value = weight_ref[:, pl.ds(at, HALF)]
        for to in range(out_ref.shape[0]):
            out_ref[to, :, part * HALF : (part + 1) * HALF] = value


def share(side, weight, count):
    return pl.pallas_call(
        share_kernel,
        in_specs=[SMEM, pl.BlockSpec(memory_space=pltpu.VMEM)],
        out_shape=jax.ShapeDtypeStruct((count, weight.shape[0], 3 * HALF), BF),
        compiler_params=params(8),
        name="share",
    )(side, weight)


def norm_kernel(code_ref, turn_ref, tokens_ref, gain_ref, _, normed_ref, extra_ref):
    xf = tokens_ref[...].astype(F32)
    scale = lax.rsqrt(jnp.mean(xf * xf, axis=-1, keepdims=True) + EPS)
    normed = xf * scale * gain_ref[...].astype(F32)
    normed_ref[...] = turned(normed, (128 - turn_ref[0]) % 128).astype(BF)
    mean = jnp.mean(xf, axis=0, keepdims=True)
    rows = jnp.concatenate([mean[:, j * 128 : (j + 1) * 128] for j in range(8)], axis=0)
    high = rows.astype(BF).astype(F32)
    mid = (rows - high).astype(BF).astype(F32)
    low = rows - high - mid
    code = jnp.full((8, 128), code_ref[0], jnp.int32).astype(F32)
    extra_ref[:, :128] = jnp.concatenate([high, mid], axis=0).astype(BF)
    extra_ref[:, 128:] = jnp.concatenate([low, code], axis=0).astype(BF)


def gathered(refs):
    own, *rest = refs
    half = rest[0].shape[0]
    after, across, before = (rest[i : i + 2] for i in range(0, 6, 2))
    rows = []
    for far in range(2 * half):
        part, at = (far // half, far % half)
        rows += [own[far], after[part][at], across[part][at], before[part][at]]
    return jnp.concatenate(rows, axis=0)


def grouped_rows(value):
    value = value.reshape(FRAMES, GROUPS, 8, value.shape[-1])
    return jnp.concatenate([value[:, g].reshape(128, -1) for g in range(GROUPS)], axis=0)


def frame_of(row):
    return row % 8 * 2 + row // 8


def causal_same_patch():
    row, col = (iota((128, 128), 0), iota((128, 128), 1))
    return (row % 8 == col % 8) & (frame_of(col // 8) <= frame_of(row // 8))


def head_masks():
    lane = iota((1, 128), 1)
    return tuple(jnp.where(lane // HEAD_DIM == j, 1.0, 0.0).astype(BF) for j in range(2))


def by_head(value, masks):
    return jnp.concatenate([value * mask for mask in masks], axis=0)


def units():
    return [(pair, group, pair * GROUPS + group) for pair in range(2) for group in range(GROUPS)]


def forward_heads(x_ref, weight_refs, qkv_ref, prob_ref):
    x = x_ref[...].reshape(ROWS, D)
    for part in range(3):
        weight = gathered(weight_refs[part * PIECES : (part + 1) * PIECES])
        qkv_ref[part] = grouped_rows(nn(x, weight)).astype(BF)
    allowed = causal_same_patch()
    masks = head_masks()

    def taken(part, pair, group):
        return qkv_ref[part, pl.ds(group * 128, 128), pl.ds(pair * 128, 128)]

    for pair, group, unit in units():
        scores = nt(by_head(taken(0, pair, group), masks), taken(1, pair, group))
        for j in range(2):
            one = scores[j * 128 : (j + 1) * 128] * HEAD_DIM ** (-0.5)
            prob_ref[unit * 2 + j] = jnp.where(allowed, one, -1e30)
    for at in range(16):
        scores = prob_ref[at]
        raised = jnp.exp(scores - jnp.max(scores, axis=1, keepdims=True))
        prob_ref[at] = raised * (1.0 / jnp.sum(raised, axis=1, keepdims=True))
    totals = [jnp.zeros((FRAMES, 128), F32)] * 2
    for pair, group, unit in units():
        weights = jnp.concatenate([prob_ref[unit * 2 + j] for j in range(2)], axis=1).astype(BF)
        mixed = nn(weights, by_head(taken(2, pair, group), masks))
        attended = mixed.astype(BF).astype(F32)
        totals[pair] = totals[pair] + jnp.sum(attended.reshape(FRAMES, 8, 128), axis=1)
    return jnp.concatenate(totals, axis=1)


def forward_kernel(_, __, side_ref, same_ref, cross_ref, *refs):
    extra_ref, qkv_ref, prob_ref, out_ref, x_ref, sum_ref = refs[3 * PIECES :]
    step = pl.program_id(0)

    @pl.when(step == 0)
    def _():
        x_ref[side_ref[0]] = same_ref[...]
        x_ref[1 - side_ref[0]] = cross_ref[...]

    lanes = pl.ds(pl.multiple_of(step * 256, 256), 256)
    sum_ref[:, lanes] = forward_heads(x_ref, refs[: 3 * PIECES], qkv_ref, prob_ref)

    @pl.when(step == 1)
    def _():
        sums = sum_ref[...].astype(BF)
        for to in range(FRAMES):
            out_ref[to, :, :HALF] = sums
            out_ref[to, :, HALF:] = extra_ref[...]


def weight_specs(weight):
    return [
        pl.BlockSpec((*piece.shape[:2], 256), lambda i, part=part: (0, 0, part * 2 + i))
        for part in range(3)
        for piece in weight
    ]


def whole(shape):
    return pl.BlockSpec(shape, lambda *_: (0,) * len(shape))


SAVED_SHAPES = (
    pltpu.HBM((3, ROWS, HALF), BF),
    pltpu.HBM((32, 128, 128), F32),
)


def saved_specs():
    return [
        pl.BlockSpec((3, ROWS, 256), lambda i: (0, 0, i)),
        pl.BlockSpec((16, 128, 128), lambda i: (i, 0, 0)),
    ]


def in_hbm(*values):
    return [pltpu.with_memory_space_constraint(v, pltpu.HBM) for v in values]


def forward(ready, ready_too, side, same, cross, weight, extra):
    return pl.pallas_call(
        forward_kernel,
        grid=(2,),
        in_specs=[
            *[pl.BlockSpec(memory_space=pl.ANY)] * 2,
            SMEM,
            whole(same.shape),
            whole(cross.shape),
            *weight_specs(weight),
            whole((16, EXTRA)),
        ],
        out_specs=[*saved_specs(), whole((16, 16, HALF + EXTRA))],
        out_shape=(*SAVED_SHAPES, pltpu.HBM((16, 16, HALF + EXTRA), BF)),
        scratch_shapes=[pltpu.VMEM((2, 8, 32, D), BF), pltpu.VMEM((FRAMES, HALF), F32)],
        compiler_params=params(24),
        cost_estimate=cost(1_000),
        name="forward",
    )(ready, ready_too, side, same, cross, *weight * 3, extra)


def head_kernel(
    at_ref, got_ref, out_w_hbm, pair_hbm, book_ref, rows_ref, mean_ref, send_ref, *scratch
):
    pooled_ref, out_w_ref, pair_ref, sem = scratch
    copies = [
        pltpu.make_async_copy(out_w_hbm, out_w_ref, sem.at[0]),
        pltpu.make_async_copy(pair_hbm, pair_ref, sem.at[1]),
    ]
    for copy in copies:
        copy.start()
    got = got_ref[...].reshape(8, 2, 16, HALF + EXTRA)
    sums = [jnp.sum(got[:, c, :, :HALF].astype(F32), axis=0) for c in range(2)]
    sums = jnp.concatenate(sums, axis=1)
    got = got.reshape(16, 16, HALF + EXTRA)
    first = got[:, :, HALF : HALF + 128].reshape(256, 128)
    second = got[:, :, HALF + 128 :].reshape(256, 128)
    row, col = (iota((128, 256), 0), iota((128, 256), 1))
    frame, piece = (frame_of(row % 16), row // 16)
    same = col // 16 == frame
    pick_two = jnp.where(same & (col % 8 == piece), 1.0, 0.0).astype(BF)
    pick_one = jnp.where(same & (col % 16 == piece), 1.0, 0.0).astype(BF)
    means = nn(pick_two, first) + nn(pick_one, second)
    xmean = jnp.concatenate([means[j * 16 : (j + 1) * 16] for j in range(8)], axis=1)
    row, col = (iota((16, 256), 0), iota((16, 256), 1))
    pick_code = jnp.where(col == frame_of(row) * 16 + 8, 1.0, 0.0).astype(BF)
    code = nn(pick_code, second)
    for copy in copies:
        copy.wait()
    sums = jnp.concatenate(two_terms(sums), axis=0)
    moved = nn(sums, out_w_ref[...])
    pooled = xmean + (moved[:FRAMES] + moved[FRAMES:]) / PATCHES
    now = nt(pooled, pair_ref[0], HIGHEST)
    later = nt(pooled, pair_ref[1], HIGHEST)
    zero = jnp.zeros((1, LATENT), F32)
    action = now + jnp.concatenate([later[8:], later[1:8], zero], axis=0)
    quantized = jnp.zeros((FRAMES, LATENT), F32)
    for k in range(CODES):
        quantized = quantized + jnp.where(code[:, :LATENT] == k, book_ref[k : k + 1, :], 0.0)
    d_action = 2.0 * BETA * (action - quantized)
    d_before = jnp.concatenate([zero, d_action[8:15], d_action[:8]], axis=0)
    d_mean = nn(d_action, pair_ref[0], HIGHEST) + nn(d_before, pair_ref[1], HIGHEST)
    mean_ref[...] = d_mean
    terms = jnp.concatenate(two_terms(d_mean), axis=0)
    both = nt(terms, out_w_ref[...])
    rows_ref[...] = (both[:FRAMES] + both[FRAMES:]).astype(BF)
    pooled_ref[...] = pooled
    mine = pooled_ref[:, pl.ds(pl.multiple_of(at_ref[0] * 128, 128), 128)]
    high, low = two_terms(d_action)
    others = [mine.astype(BF), high, low, code[:, : 2 * LATENT].astype(BF)]
    mine = jnp.concatenate(others, axis=1)
    for to in range(send_ref.shape[0]):
        send_ref[to] = mine


def head(at, got, out_w, w_pair, codebook, clips):
    return pl.pallas_call(
        head_kernel,
        in_specs=[
            SMEM,
            pl.BlockSpec(memory_space=pltpu.VMEM),
            *[pl.BlockSpec(memory_space=pl.ANY)] * 2,
            pl.BlockSpec(memory_space=pltpu.VMEM),
        ],
        out_shape=(
            pltpu.HBM((FRAMES, D), BF),
            pltpu.HBM((FRAMES, D), F32),
            pltpu.HBM((clips, FRAMES, 256), BF),
        ),
        scratch_shapes=[
            pltpu.VMEM((FRAMES, D), F32),
            pltpu.VMEM((D, D), BF),
            pltpu.VMEM((2, LATENT, D), F32),
            pltpu.SemaphoreType.DMA((2,)),
        ],
        compiler_params=params(16),
        cost_estimate=cost(1_000),
        name="head",
    )(at, got, *in_hbm(out_w, w_pair), codebook)


def backward_heads(rows_ref, at, qkv_ref, prob_ref, weight_refs, acc_ref, cot_ref, part_ref):
    masks = head_masks()
    d_frames = rows_ref[:, pl.ds(at, 256)].astype(F32)
    d_all = jnp.broadcast_to(d_frames[:, None, :], (FRAMES, 8, 256)).reshape(128, 256).astype(BF)
    d_heads = [by_head(d_all[:, pair * 128 : (pair + 1) * 128], masks) for pair in range(2)]

    def taken(part, pair, group):
        return qkv_ref[part, pl.ds(group * 128, 128), pl.ds(pair * 128, 128)]

    for pair, group, unit in units():
        d_weights = nt(d_heads[pair], taken(2, pair, group))
        for j in range(2):
            cot_ref[unit * 2 + j] = d_weights[j * 128 : (j + 1) * 128].astype(BF)
    for index in range(16):
        prob = prob_ref[index]
        d_weights = cot_ref[index].astype(F32)
        inner = jnp.sum(d_weights * prob, axis=1, keepdims=True)
        cot_ref[index] = (prob * (d_weights - inner) * HEAD_DIM ** (-0.5)).astype(BF)
    for pair, group, unit in units():
        d_scores = [cot_ref[unit * 2 + j] for j in range(2)]
        prob = jnp.concatenate([prob_ref[unit * 2 + j].astype(BF) for j in range(2)], axis=0)
        d_query = nn(jnp.concatenate(d_scores, axis=1), by_head(taken(1, pair, group), masks))
        d_keys = tn(jnp.concatenate(d_scores, axis=0), by_head(taken(0, pair, group), masks))
        d_values = tn(prob, d_heads[pair])
        for part, value in enumerate((d_query, d_keys, d_values)):
            part_ref[part, pl.ds(group * 128, 128), pl.ds(pair * 128, 128)] = value.astype(BF)
    total = None
    for part in range(3):
        term = nt(part_ref[part], gathered(weight_refs[part * PIECES : (part + 1) * PIECES]))
        total = term if total is None else total + term
    acc_ref[...] += total


def backward_kernel(side_ref, rows_ref, *refs):
    keep_ref, give_ref, acc_ref, parts_ref, *scratch = refs[2 + 3 * PIECES :]
    step = pl.program_id(0)
    side = side_ref[0]

    @pl.when(step == 0)
    def _():
        acc_ref[...] = jnp.zeros_like(acc_ref)

    at = pl.multiple_of(side * HALF + step * 256, 256)
    backward_heads(rows_ref, at, refs[0], refs[1], refs[2 : 2 + 3 * PIECES], acc_ref, *scratch)

    @pl.when(step == 1)
    def _():
        for group in range(GROUPS):
            rows = acc_ref[pl.ds(group * 128, 128), :].reshape(2, 8, 8, D)
            parts_ref[:, :, pl.ds(group * 8, 8), :] = rows
        keep_ref[...] = parts_ref[side]
        give_ref[...] = parts_ref[1 - side].astype(BF)


def backward(side, d_rows, qkv, prob, weight):
    return pl.pallas_call(
        backward_kernel,
        grid=(2,),
        in_specs=[SMEM, whole((FRAMES, D)), *saved_specs(), *weight_specs(weight)],
        out_specs=[whole((8, 32, D))] * 2,
        out_shape=(pltpu.HBM((8, 32, D), F32), jax.ShapeDtypeStruct((8, 32, D), BF)),
        scratch_shapes=[
            pltpu.VMEM((ROWS, D), F32),
            pltpu.VMEM((2, 8, 32, D), F32),
            pltpu.VMEM((16, 128, 128), BF),
            pltpu.VMEM((3, ROWS, 256), BF),
        ],
        compiler_params=params(32),
        cost_estimate=cost(1_000),
        name="backward",
    )(side, *in_hbm(d_rows, qkv, prob), *weight * 3)


def grads_kernel(_, keep_ref, cross_ref, got_ref, out_ref, step_ref):
    count = got_ref.shape[0] * FRAMES
    got = got_ref[...].reshape(count, 256)
    means, others = (got[:, :128], got[:, 128:])
    wide = others.astype(F32)
    place, lane = (iota((count, 128), 0) % FRAMES, iota((count, 128), 1))
    shift = jnp.where(place == 0, 0.0, pltpu.roll(wide, count - 7, 0))
    before = jnp.where(place >= 8, pltpu.roll(wide, 8, 0), shift).astype(BF)
    code = wide[:, 2 * LATENT : 2 * LATENT + 1]
    onehot = jnp.where((code == lane.astype(F32)) & (lane < CODES), 1.0, 0.0).astype(BF)
    for part, value in enumerate((others, before)):
        terms = tn(value, means)
        total = (terms[:LATENT] + terms[LATENT : 2 * LATENT]).astype(BF)
        for to in range(8):
            out_ref[to, :, D + part * 128 : D + (part + 1) * 128] = total
    counted = jnp.where(lane < 2 * LATENT, wide, 1.0).astype(BF)
    totals = tn(onehot, counted)[:CODES]
    by_code = (totals[:, :LATENT] + totals[:, LATENT : 2 * LATENT]) * (-1.0 / BETA)
    out_ref[:, :, :D] = (keep_ref[...] + cross_ref[...].astype(F32)).astype(BF)
    step_ref[...] = by_code / totals[:, 2 * LATENT : 2 * LATENT + 1]


def grads(ready, keep, cross, got):
    return pl.pallas_call(
        grads_kernel,
        in_specs=[pl.BlockSpec(memory_space=pl.ANY), *[pl.BlockSpec(memory_space=pltpu.VMEM)] * 3],
        out_shape=(
            pltpu.HBM((8, 32, D + GRADS), BF),
            jax.ShapeDtypeStruct((CODES, LATENT), F32),
        ),
        compiler_params=params(8),
        cost_estimate=cost(1_000),
        name="grads",
    )(ready, keep, cross, got)


def last_kernel(at_ref, turn_ref, got_ref, tokens_ref, gain_ref, mean_ref, out_ref, pair_ref):
    xf = tokens_ref[...].astype(F32)
    scale = lax.rsqrt(jnp.mean(xf * xf, axis=-1, keepdims=True) + EPS)
    d_normed = turned(got_ref[:, :, :D].reshape(xf.shape).astype(F32), turn_ref[0])
    d_scaled = d_normed * gain_ref[...].astype(F32)
    inner = jnp.sum(d_scaled * xf, axis=-1, keepdims=True) / D
    d_through = d_scaled * scale - xf * (scale * scale * scale * inner)
    d_resid = mean_ref[pl.ds(at_ref[0], 1), :]
    out_ref[...] = (d_resid + d_through).astype(BF)
    for t in range(2):
        for part in range(2):
            value = got_ref[t, :, pl.ds(D + part * 128, 128)]
            pair_ref[part, :, pl.ds(t * 128, 128)] = value.astype(F32)


def last(at, turn, got, tokens, gain, d_mean):
    return pl.pallas_call(
        last_kernel,
        grid=(4,),
        in_specs=[
            SMEM,
            SMEM,
            pl.BlockSpec((2, 32, D + GRADS), lambda i: (i, 0, 0)),
            pl.BlockSpec((64, D), lambda i: (i, 0)),
            whole((1, D)),
            whole((FRAMES, D)),
        ],
        out_specs=[
            pl.BlockSpec((64, D), lambda i: (i, 0)),
            pl.BlockSpec((2, LATENT, 256), lambda i: (0, 0, i)),
        ],
        out_shape=(
            jax.ShapeDtypeStruct((PATCHES, D), BF),
            jax.ShapeDtypeStruct((2, LATENT, D), F32),
        ),
        compiler_params=params(8),
        name="last",
    )(at, turn, got, tokens, gain, d_mean)


def cost(flops):
    return pl.CostEstimate(flops=flops, transcendentals=0, bytes_accessed=0)


def touch_kernel(*refs):
    refs[-1][...] = jnp.zeros_like(refs[-1])


def touched(flops, *values):
    return pl.pallas_call(
        touch_kernel,
        in_specs=[pl.BlockSpec(memory_space=pltpu.VMEM)] * len(values),
        out_shape=pltpu.HBM((8, 128), F32),
        compiler_params=params(4),
        cost_estimate=cost(flops),
        name="touch",
    )(*values)


def shifted(value, axis, by):
    count = lax.axis_size(axis)
    return lax.ppermute(value, axis, [(i, (i + by) % count) for i in range(count)])


def local(tokens, gain, w_qkv, w_out, w_pair, codebook, codes):
    side = lax.axis_index("tm_1")
    layer = lax.axis_index("tm_0")
    turn = (lax.axis_index("dp_1") * 32).reshape(1)
    rows = w_qkv.shape[0]
    tokens = tokens.reshape(PATCHES, D)
    gain = gain.reshape(1, D)
    full_out = lax.all_gather(w_out, DP, axis=0, tiled=True)
    far = lax.axis_size("dp_0")
    near = lax.all_to_all(share(side.reshape(1), w_qkv, far), "dp_0", 0, 0, tiled=True)
    half = near.shape[0] // 2
    early, late = (near[:half], near[half:])
    before_early = shifted(early, "dp_1", 1)
    after_late = shifted(late, "dp_1", -1)
    first = shifted(before_early, "dp_1", 1)
    second = shifted(after_late, "dp_1", -1)
    after = [shifted(early, "dp_1", -1), after_late]
    before = [before_early, shifted(late, "dp_1", 1)]
    own_w = [near, *after, first, second, *before]
    at = (side * 8 + layer).reshape(1)
    layer = layer.reshape(1)
    side = side.reshape(1)

    normed, extra = pl.pallas_call(
        norm_kernel,
        in_specs=[
            SMEM,
            SMEM,
            *[pl.BlockSpec(memory_space=pltpu.VMEM)] * 2,
            pl.BlockSpec(memory_space=pl.ANY),
        ],
        out_shape=(
            pltpu.HBM((PATCHES, D), BF),
            jax.ShapeDtypeStruct((16, EXTRA), BF),
        ),
        compiler_params=params(8),
        cost_estimate=cost(1_000),
        name="norm",
    )(codes.reshape(1), turn, tokens, gain, near)
    same = lax.all_to_all(normed.reshape(8, 32, D), "tm_0", 0, 0, tiled=True)
    cross = shifted(same, "tm_1", 1)
    qkv, prob, partial = forward(touched(10_000_000_000, first, second), touched(10_000_000_000, after[0], before[1]), side, same, cross, own_w, extra)
    arrived = lax.all_to_all(partial, TM, 0, 0, tiled=True)
    clips = lax.axis_size(DP)
    pair = jnp.swapaxes(w_pair, 1, 2)
    d_rows, d_mean, mine = head(layer, arrived, full_out, pair, codebook, clips)
    everyone = lax.all_to_all(mine, DP, 0, 0, tiled=True)
    keep, give = backward(side, d_rows, qkv, prob, own_w)
    ready = touched(1_000_000_000, everyone)
    outgoing, codebook_step = grads(ready, keep, shifted(give, "tm_1", 1), everyone)
    back = lax.all_to_all(outgoing, "tm_0", 0, 0, tiled=True)
    grad_tokens, grad_pair = last(at, turn, back, tokens, gain, d_mean)
    return (
        grad_tokens.reshape(1, 1, PATCHES, D),
        jnp.swapaxes(grad_pair, 1, 2),
        codebook_step,
    )


def solution(mesh):
    torus = Mesh(mesh.devices.reshape(8, 4, 8, 2), ("dp_0", "dp_1", "tm_0", "tm_1"))
    return jax.shard_map(
        local,
        mesh=torus,
        in_specs=(P(DP, TM, None, None), P(), P(DP, None), P(DP, None), P(), P(), P(DP, TM, None)),
        out_specs=(P(DP, TM, None, None), P(), P()),
        check_vma=False,
    )
```

```python
import jax
import jax.numpy as jnp
from jax import lax
from jax.experimental import pallas as pl
from jax.experimental.pallas import tpu as pltpu
from jax.sharding import Mesh
from jax.sharding import PartitionSpec as P

D = 1024
HEAD_DIM = 64
LATENT = 32
CODES = 8
PATCHES = 256
FRAMES = 16
EPS = 1e-06
BETA = 0.25
DP = ("dp_0", "dp_1")
TM = ("tm_0", "tm_1")
HALF = 512
EXTRA = 256
GRADS = 256
PIECES = 7
GROUPS = 4
ROWS = 512
BF = jnp.bfloat16
F32 = jnp.float32
HIGHEST = lax.Precision.HIGHEST


def params(mebibytes):
    return pltpu.CompilerParams(vmem_limit_bytes=mebibytes * 1024 * 1024)


SMEM = pl.BlockSpec(memory_space=pltpu.SMEM)


def nn(a, b, precision=None):
    return lax.dot_general(
        a, b, (((1,), (0,)), ((), ())), precision=precision, preferred_element_type=F32
    )


def nt(a, b, precision=None):
    return lax.dot_general(
        a, b, (((1,), (1,)), ((), ())), precision=precision, preferred_element_type=F32
    )


def tn(a, b, precision=None):
    return lax.dot_general(
        a, b, (((0,), (0,)), ((), ())), precision=precision, preferred_element_type=F32
    )


def two_terms(value):
    high = value.astype(BF)
    return high, (value - high.astype(F32)).astype(BF)


def iota(shape, dim):
    return lax.broadcasted_iota(jnp.int32, shape, dim)


def turned(value, shift):
    width = value.shape[-1]
    tiles = [pltpu.roll(value[:, j : j + 128], shift, 1) for j in range(0, width, 128)]
    return jnp.concatenate(tiles, axis=1)


def share_kernel(side_ref, weight_ref, out_ref, own_ref, sem):
    copies = []
    for part in range(3):
        at = pl.multiple_of(part * D + side_ref[0] * HALF, HALF)
        lanes = pl.ds(part * HALF, HALF)
        piece = weight_ref.at[:, pl.ds(at, HALF)]
        copies.append(pltpu.make_async_copy(piece, own_ref.at[:, lanes], sem.at[part]))
    for copy in copies:
        copy.start()
    for copy in copies:
        copy.wait()
    sends = [
        pltpu.make_async_copy(own_ref, out_ref.at[to], sem.at[3 + to])
        for to in range(out_ref.shape[0])
    ]
    for send in sends:
        send.start()
    for send in sends:
        send.wait()


def share(side, weight, count):
    rows = weight.shape[0]
    return pl.pallas_call(
        share_kernel,
        in_specs=[SMEM, pl.BlockSpec(memory_space=pl.ANY)],
        out_specs=pl.BlockSpec(memory_space=pl.ANY),
        out_shape=pltpu.HBM((count, rows, 3 * HALF), BF),
        scratch_shapes=[
            pltpu.VMEM((rows, 3 * HALF), BF),
            pltpu.SemaphoreType.DMA((3 + count,)),
        ],
        compiler_params=params(8),
        name="share",
    )(side, *in_hbm(weight))


def norm_kernel(code_ref, turn_ref, tokens_ref, gain_ref, _, normed_ref, extra_ref):
    xf = tokens_ref[...].astype(F32)
    scale = lax.rsqrt(jnp.mean(xf * xf, axis=-1, keepdims=True) + EPS)
    normed = xf * scale * gain_ref[...].astype(F32)
    normed_ref[...] = turned(normed, (128 - turn_ref[0]) % 128).astype(BF)
    mean = jnp.mean(xf, axis=0, keepdims=True)
    rows = jnp.concatenate([mean[:, j * 128 : (j + 1) * 128] for j in range(8)], axis=0)
    high = rows.astype(BF).astype(F32)
    mid = (rows - high).astype(BF).astype(F32)
    low = rows - high - mid
    code = jnp.full((8, 128), code_ref[0], jnp.int32).astype(F32)
    extra_ref[:, :128] = jnp.concatenate([high, mid], axis=0).astype(BF)
    extra_ref[:, 128:] = jnp.concatenate([low, code], axis=0).astype(BF)


def gathered(refs):
    own, *rest = refs
    half = rest[0].shape[0]
    after, across, before = (rest[i : i + 2] for i in range(0, 6, 2))
    rows = []
    for far in range(2 * half):
        part, at = (far // half, far % half)
        rows += [own[far], after[part][at], across[part][at], before[part][at]]
    return jnp.concatenate(rows, axis=0)


def grouped_rows(value):
    value = value.reshape(FRAMES, GROUPS, 8, value.shape[-1])
    return jnp.concatenate([value[:, g].reshape(128, -1) for g in range(GROUPS)], axis=0)


def frame_of(row):
    return row % 8 * 2 + row // 8


def causal_same_patch():
    row, col = (iota((128, 128), 0), iota((128, 128), 1))
    return (row % 8 == col % 8) & (frame_of(col // 8) <= frame_of(row // 8))


def head_masks():
    lane = iota((1, 128), 1)
    return tuple(jnp.where(lane // HEAD_DIM == j, 1.0, 0.0).astype(BF) for j in range(2))


def by_head(value, masks):
    return jnp.concatenate([value * mask for mask in masks], axis=0)


def units():
    return [(pair, group, pair * GROUPS + group) for pair in range(2) for group in range(GROUPS)]


def forward_heads(x_ref, weight_refs, qkv_ref, prob_ref):
    x = x_ref[...].reshape(ROWS, D)
    for part in range(3):
        weight = gathered(weight_refs[part * PIECES : (part + 1) * PIECES])
        qkv_ref[part] = grouped_rows(nn(x, weight)).astype(BF)
    allowed = causal_same_patch()
    masks = head_masks()

    def taken(part, pair, group):
        return qkv_ref[part, pl.ds(group * 128, 128), pl.ds(pair * 128, 128)]

    for pair, group, unit in units():
        scores = nt(by_head(taken(0, pair, group), masks), taken(1, pair, group))
        for j in range(2):
            one = scores[j * 128 : (j + 1) * 128] * HEAD_DIM ** (-0.5)
            prob_ref[unit * 2 + j] = jnp.where(allowed, one, -1e30)
    for at in range(16):
        scores = prob_ref[at]
        raised = jnp.exp(scores - jnp.max(scores, axis=1, keepdims=True))
        prob_ref[at] = raised * (1.0 / jnp.sum(raised, axis=1, keepdims=True))
    totals = [jnp.zeros((FRAMES, 128), F32)] * 2
    for pair, group, unit in units():
        weights = jnp.concatenate([prob_ref[unit * 2 + j] for j in range(2)], axis=1).astype(BF)
        mixed = nn(weights, by_head(taken(2, pair, group), masks))
        attended = mixed.astype(BF).astype(F32)
        totals[pair] = totals[pair] + jnp.sum(attended.reshape(FRAMES, 8, 128), axis=1)
    return jnp.concatenate(totals, axis=1)


def forward_kernel(_, __, side_ref, same_ref, cross_ref, *refs):
    extra_ref, qkv_ref, prob_ref, out_ref, x_ref, sum_ref = refs[3 * PIECES :]
    step = pl.program_id(0)

    @pl.when(step == 0)
    def _():
        x_ref[side_ref[0]] = same_ref[...]
        x_ref[1 - side_ref[0]] = cross_ref[...]

    lanes = pl.ds(pl.multiple_of(step * 256, 256), 256)
    sum_ref[:, lanes] = forward_heads(x_ref, refs[: 3 * PIECES], qkv_ref, prob_ref)

    @pl.when(step == 1)
    def _():
        sums = sum_ref[...].astype(BF)
        for to in range(FRAMES):
            out_ref[to, :, :HALF] = sums
            out_ref[to, :, HALF:] = extra_ref[...]


def weight_specs(weight):
    return [
        pl.BlockSpec((*piece.shape[:2], 256), lambda i, part=part: (0, 0, part * 2 + i))
        for part in range(3)
        for piece in weight
    ]


def whole(shape):
    return pl.BlockSpec(shape, lambda *_: (0,) * len(shape))


SAVED_SHAPES = (
    pltpu.HBM((3, ROWS, HALF), BF),
    pltpu.HBM((32, 128, 128), F32),
)


def saved_specs():
    return [
        pl.BlockSpec((3, ROWS, 256), lambda i: (0, 0, i)),
        pl.BlockSpec((16, 128, 128), lambda i: (i, 0, 0)),
    ]


def in_hbm(*values):
    return [pltpu.with_memory_space_constraint(v, pltpu.HBM) for v in values]


def forward(ready, ready_too, side, same, cross, weight, extra):
    return pl.pallas_call(
        forward_kernel,
        grid=(2,),
        in_specs=[
            *[pl.BlockSpec(memory_space=pl.ANY)] * 2,
            SMEM,
            whole(same.shape),
            whole(cross.shape),
            *weight_specs(weight),
            whole((16, EXTRA)),
        ],
        out_specs=[*saved_specs(), whole((16, 16, HALF + EXTRA))],
        out_shape=(*SAVED_SHAPES, pltpu.HBM((16, 16, HALF + EXTRA), BF)),
        scratch_shapes=[pltpu.VMEM((2, 8, 32, D), BF), pltpu.VMEM((FRAMES, HALF), F32)],
        compiler_params=params(24),
        cost_estimate=cost(1_000),
        name="forward",
    )(*in_hbm(ready, ready_too), side, same, cross, *weight * 3, extra)


def head_kernel(
    at_ref, got_ref, out_w_hbm, pair_hbm, book_ref, rows_ref, mean_ref, send_ref, *scratch
):
    pooled_ref, out_w_ref, pair_ref, sem = scratch
    copies = [
        pltpu.make_async_copy(out_w_hbm, out_w_ref, sem.at[0]),
        pltpu.make_async_copy(pair_hbm, pair_ref, sem.at[1]),
    ]
    for copy in copies:
        copy.start()
    got = got_ref[...].reshape(8, 2, 16, HALF + EXTRA)
    sums = [jnp.sum(got[:, c, :, :HALF].astype(F32), axis=0) for c in range(2)]
    sums = jnp.concatenate(sums, axis=1)
    got = got.reshape(16, 16, HALF + EXTRA)
    first = got[:, :, HALF : HALF + 128].reshape(256, 128)
    second = got[:, :, HALF + 128 :].reshape(256, 128)
    row, col = (iota((128, 256), 0), iota((128, 256), 1))
    frame, piece = (frame_of(row % 16), row // 16)
    same = col // 16 == frame
    pick_two = jnp.where(same & (col % 8 == piece), 1.0, 0.0).astype(BF)
    pick_one = jnp.where(same & (col % 16 == piece), 1.0, 0.0).astype(BF)
    means = nn(pick_two, first) + nn(pick_one, second)
    xmean = jnp.concatenate([means[j * 16 : (j + 1) * 16] for j in range(8)], axis=1)
    row, col = (iota((16, 256), 0), iota((16, 256), 1))
    pick_code = jnp.where(col == frame_of(row) * 16 + 8, 1.0, 0.0).astype(BF)
    code = nn(pick_code, second)
    for copy in copies:
        copy.wait()
    sums = jnp.concatenate(two_terms(sums), axis=0)
    moved = nn(sums, out_w_ref[...])
    pooled = xmean + (moved[:FRAMES] + moved[FRAMES:]) / PATCHES
    now = nt(pooled, pair_ref[0], HIGHEST)
    later = nt(pooled, pair_ref[1], HIGHEST)
    zero = jnp.zeros((1, LATENT), F32)
    action = now + jnp.concatenate([later[8:], later[1:8], zero], axis=0)
    quantized = jnp.zeros((FRAMES, LATENT), F32)
    for k in range(CODES):
        quantized = quantized + jnp.where(code[:, :LATENT] == k, book_ref[k : k + 1, :], 0.0)
    d_action = 2.0 * BETA * (action - quantized)
    d_before = jnp.concatenate([zero, d_action[8:15], d_action[:8]], axis=0)
    d_mean = nn(d_action, pair_ref[0], HIGHEST) + nn(d_before, pair_ref[1], HIGHEST)
    mean_ref[...] = d_mean
    terms = jnp.concatenate(two_terms(d_mean), axis=0)
    both = nt(terms, out_w_ref[...])
    rows_ref[...] = (both[:FRAMES] + both[FRAMES:]).astype(BF)
    pooled_ref[...] = pooled
    mine = pooled_ref[:, pl.ds(pl.multiple_of(at_ref[0] * 128, 128), 128)]
    high, low = two_terms(d_action)
    others = [mine.astype(BF), high, low, code[:, : 2 * LATENT].astype(BF)]
    mine = jnp.concatenate(others, axis=1)
    for to in range(send_ref.shape[0]):
        send_ref[to] = mine


def head(at, got, out_w, w_pair, codebook, clips):
    return pl.pallas_call(
        head_kernel,
        in_specs=[
            SMEM,
            pl.BlockSpec(memory_space=pltpu.VMEM),
            *[pl.BlockSpec(memory_space=pl.ANY)] * 2,
            pl.BlockSpec(memory_space=pltpu.VMEM),
        ],
        out_shape=(
            pltpu.HBM((FRAMES, D), BF),
            pltpu.HBM((FRAMES, D), F32),
            pltpu.HBM((clips, FRAMES, 256), BF),
        ),
        scratch_shapes=[
            pltpu.VMEM((FRAMES, D), F32),
            pltpu.VMEM((D, D), BF),
            pltpu.VMEM((2, LATENT, D), F32),
            pltpu.SemaphoreType.DMA((2,)),
        ],
        compiler_params=params(16),
        cost_estimate=cost(1_000),
        name="head",
    )(at, got, *in_hbm(out_w, w_pair), codebook)


def backward_heads(rows_ref, at, qkv_ref, prob_ref, weight_refs, acc_ref, cot_ref, part_ref):
    masks = head_masks()
    d_frames = rows_ref[:, pl.ds(at, 256)].astype(F32)
    d_all = jnp.broadcast_to(d_frames[:, None, :], (FRAMES, 8, 256)).reshape(128, 256).astype(BF)
    d_heads = [by_head(d_all[:, pair * 128 : (pair + 1) * 128], masks) for pair in range(2)]

    def taken(part, pair, group):
        return qkv_ref[part, pl.ds(group * 128, 128), pl.ds(pair * 128, 128)]

    for pair, group, unit in units():
        d_weights = nt(d_heads[pair], taken(2, pair, group))
        for j in range(2):
            cot_ref[unit * 2 + j] = d_weights[j * 128 : (j + 1) * 128].astype(BF)
    for index in range(16):
        prob = prob_ref[index]
        d_weights = cot_ref[index].astype(F32)
        inner = jnp.sum(d_weights * prob, axis=1, keepdims=True)
        cot_ref[index] = (prob * (d_weights - inner) * HEAD_DIM ** (-0.5)).astype(BF)
    for pair, group, unit in units():
        d_scores = [cot_ref[unit * 2 + j] for j in range(2)]
        prob = jnp.concatenate([prob_ref[unit * 2 + j].astype(BF) for j in range(2)], axis=0)
        d_query = nn(jnp.concatenate(d_scores, axis=1), by_head(taken(1, pair, group), masks))
        d_keys = tn(jnp.concatenate(d_scores, axis=0), by_head(taken(0, pair, group), masks))
        d_values = tn(prob, d_heads[pair])
        for part, value in enumerate((d_query, d_keys, d_values)):
            part_ref[part, pl.ds(group * 128, 128), pl.ds(pair * 128, 128)] = value.astype(BF)
    total = None
    for part in range(3):
        term = nt(part_ref[part], gathered(weight_refs[part * PIECES : (part + 1) * PIECES]))
        total = term if total is None else total + term
    acc_ref[...] += total


def backward_kernel(side_ref, rows_ref, *refs):
    keep_ref, give_ref, acc_ref, parts_ref, *scratch = refs[2 + 3 * PIECES :]
    step = pl.program_id(0)
    side = side_ref[0]

    @pl.when(step == 0)
    def _():
        acc_ref[...] = jnp.zeros_like(acc_ref)

    at = pl.multiple_of(side * HALF + step * 256, 256)
    backward_heads(rows_ref, at, refs[0], refs[1], refs[2 : 2 + 3 * PIECES], acc_ref, *scratch)

    @pl.when(step == 1)
    def _():
        for group in range(GROUPS):
            rows = acc_ref[pl.ds(group * 128, 128), :].reshape(2, 8, 8, D)
            parts_ref[:, :, pl.ds(group * 8, 8), :] = rows
        keep_ref[...] = parts_ref[side]
        give_ref[...] = parts_ref[1 - side].astype(BF)


def backward(side, d_rows, qkv, prob, weight):
    return pl.pallas_call(
        backward_kernel,
        grid=(2,),
        in_specs=[SMEM, whole((FRAMES, D)), *saved_specs(), *weight_specs(weight)],
        out_specs=[whole((8, 32, D))] * 2,
        out_shape=(pltpu.HBM((8, 32, D), F32), jax.ShapeDtypeStruct((8, 32, D), BF)),
        scratch_shapes=[
            pltpu.VMEM((ROWS, D), F32),
            pltpu.VMEM((2, 8, 32, D), F32),
            pltpu.VMEM((16, 128, 128), BF),
            pltpu.VMEM((3, ROWS, 256), BF),
        ],
        compiler_params=params(32),
        cost_estimate=cost(1_000),
        name="backward",
    )(side, *in_hbm(d_rows, qkv, prob), *weight * 3)


def grads_kernel(_, keep_ref, cross_ref, got_ref, out_ref, step_ref):
    count = got_ref.shape[0] * FRAMES
    got = got_ref[...].reshape(count, 256)
    means, others = (got[:, :128], got[:, 128:])
    wide = others.astype(F32)
    place, lane = (iota((count, 128), 0) % FRAMES, iota((count, 128), 1))
    shift = jnp.where(place == 0, 0.0, pltpu.roll(wide, count - 7, 0))
    before = jnp.where(place >= 8, pltpu.roll(wide, 8, 0), shift).astype(BF)
    code = wide[:, 2 * LATENT : 2 * LATENT + 1]
    onehot = jnp.where((code == lane.astype(F32)) & (lane < CODES), 1.0, 0.0).astype(BF)
    for part, value in enumerate((others, before)):
        terms = tn(value, means)
        total = (terms[:LATENT] + terms[LATENT : 2 * LATENT]).astype(BF)
        for to in range(8):
            out_ref[to, :, D + part * 128 : D + (part + 1) * 128] = total
    counted = jnp.where(lane < 2 * LATENT, wide, 1.0).astype(BF)
    totals = tn(onehot, counted)[:CODES]
    by_code = (totals[:, :LATENT] + totals[:, LATENT : 2 * LATENT]) * (-1.0 / BETA)
    out_ref[:, :, :D] = (keep_ref[...] + cross_ref[...].astype(F32)).astype(BF)
    step_ref[...] = by_code / totals[:, 2 * LATENT : 2 * LATENT + 1]


def grads(ready, keep, cross, got):
    return pl.pallas_call(
        grads_kernel,
        in_specs=[pl.BlockSpec(memory_space=pl.ANY), *[pl.BlockSpec(memory_space=pltpu.VMEM)] * 3],
        out_shape=(
            pltpu.HBM((8, 32, D + GRADS), BF),
            jax.ShapeDtypeStruct((CODES, LATENT), F32),
        ),
        compiler_params=params(8),
        cost_estimate=cost(1_000),
        name="grads",
    )(*in_hbm(ready), keep, cross, got)


def last_kernel(at_ref, turn_ref, got_ref, tokens_ref, gain_ref, mean_ref, out_ref, pair_ref):
    xf = tokens_ref[...].astype(F32)
    scale = lax.rsqrt(jnp.mean(xf * xf, axis=-1, keepdims=True) + EPS)
    d_normed = turned(got_ref[:, :, :D].reshape(xf.shape).astype(F32), turn_ref[0])
    d_scaled = d_normed * gain_ref[...].astype(F32)
    inner = jnp.sum(d_scaled * xf, axis=-1, keepdims=True) / D
    d_through = d_scaled * scale - xf * (scale * scale * scale * inner)
    d_resid = mean_ref[pl.ds(at_ref[0], 1), :]
    out_ref[...] = (d_resid + d_through).astype(BF)
    for t in range(2):
        for part in range(2):
            value = got_ref[t, :, pl.ds(D + part * 128, 128)]
            pair_ref[part, :, pl.ds(t * 128, 128)] = value.astype(F32)


def last(at, turn, got, tokens, gain, d_mean):
    return pl.pallas_call(
        last_kernel,
        grid=(4,),
        in_specs=[
            SMEM,
            SMEM,
            pl.BlockSpec((2, 32, D + GRADS), lambda i: (i, 0, 0)),
            pl.BlockSpec((64, D), lambda i: (i, 0)),
            whole((1, D)),
            whole((FRAMES, D)),
        ],
        out_specs=[
            pl.BlockSpec((64, D), lambda i: (i, 0)),
            pl.BlockSpec((2, LATENT, 256), lambda i: (0, 0, i)),
        ],
        out_shape=(
            jax.ShapeDtypeStruct((PATCHES, D), BF),
            jax.ShapeDtypeStruct((2, LATENT, D), F32),
        ),
        compiler_params=params(8),
        name="last",
    )(at, turn, got, tokens, gain, d_mean)


def cost(flops):
    return pl.CostEstimate(flops=flops, transcendentals=0, bytes_accessed=0)


def touch_kernel(*refs):
    refs[-1][...] = jnp.zeros_like(refs[-1])


def touched(flops, *values):
    return pl.pallas_call(
        touch_kernel,
        in_specs=[pl.BlockSpec(memory_space=pltpu.VMEM)] * len(values),
        out_shape=pltpu.HBM((8, 128), F32),
        compiler_params=params(4),
        cost_estimate=cost(flops),
        name="touch",
    )(*values)


def shifted(value, axis, by):
    count = lax.axis_size(axis)
    return lax.ppermute(value, axis, [(i, (i + by) % count) for i in range(count)])


def local(tokens, gain, w_qkv, w_out, w_pair, codebook, codes):
    side = lax.axis_index("tm_1")
    layer = lax.axis_index("tm_0")
    turn = (lax.axis_index("dp_1") * 32).reshape(1)
    rows = w_qkv.shape[0]
    tokens = tokens.reshape(PATCHES, D)
    gain = gain.reshape(1, D)
    full_out = lax.all_gather(w_out, DP, axis=0, tiled=True)
    far = lax.axis_size("dp_0")
    near = lax.all_to_all(share(side.reshape(1), w_qkv, far), "dp_0", 0, 0, tiled=True)
    half = near.shape[0] // 2
    early, late = (near[:half], near[half:])
    before_early = shifted(early, "dp_1", 1)
    after_late = shifted(late, "dp_1", -1)
    first = shifted(before_early, "dp_1", 1)
    second = shifted(after_late, "dp_1", -1)
    after = [shifted(early, "dp_1", -1), after_late]
    before = [before_early, shifted(late, "dp_1", 1)]
    own_w = [near, *after, first, second, *before]
    at = (side * 8 + layer).reshape(1)
    layer = layer.reshape(1)
    side = side.reshape(1)

    normed, extra = pl.pallas_call(
        norm_kernel,
        in_specs=[
            SMEM,
            SMEM,
            *[pl.BlockSpec(memory_space=pltpu.VMEM)] * 2,
            pl.BlockSpec(memory_space=pl.ANY),
        ],
        out_shape=(
            pltpu.HBM((PATCHES, D), BF),
            jax.ShapeDtypeStruct((16, EXTRA), BF),
        ),
        compiler_params=params(8),
        cost_estimate=cost(1_000),
        name="norm",
    )(codes.reshape(1), turn, tokens, gain, near)
    same = lax.all_to_all(normed.reshape(8, 32, D), "tm_0", 0, 0, tiled=True)
    cross = shifted(same, "tm_1", 1)
    qkv, prob, partial = forward(touched(10_000_000_000, first, second), touched(10_000_000_000, after[0], before[1]), side, same, cross, own_w, extra)
    arrived = lax.all_to_all(partial, TM, 0, 0, tiled=True)
    clips = lax.axis_size(DP)
    pair = jnp.swapaxes(w_pair, 1, 2)
    d_rows, d_mean, mine = head(layer, arrived, full_out, pair, codebook, clips)
    everyone = lax.all_to_all(mine, DP, 0, 0, tiled=True)
    keep, give = backward(side, d_rows, qkv, prob, own_w)
    ready = touched(1_000_000_000, everyone)
    outgoing, codebook_step = grads(ready, keep, shifted(give, "tm_1", 1), everyone)
    back = lax.all_to_all(outgoing, "tm_0", 0, 0, tiled=True)
    grad_tokens, grad_pair = last(at, turn, back, tokens, gain, d_mean)
    return (
        grad_tokens.reshape(1, 1, PATCHES, D),
        jnp.swapaxes(grad_pair, 1, 2),
        codebook_step,
    )


def solution(mesh):
    torus = Mesh(mesh.devices.reshape(8, 4, 8, 2), ("dp_0", "dp_1", "tm_0", "tm_1"))
    return jax.shard_map(
        local,
        mesh=torus,
        in_specs=(P(DP, TM, None, None), P(), P(DP, None), P(DP, None), P(), P(), P(DP, TM, None)),
        out_specs=(P(DP, TM, None, None), P(), P()),
        check_vma=False,
    )
```

```python
import jax
import jax.numpy as jnp
from jax import lax
from jax.experimental import pallas as pl
from jax.experimental.pallas import tpu as pltpu
from jax.sharding import Mesh
from jax.sharding import PartitionSpec as P

D = 1024
HEAD_DIM = 64
LATENT = 32
CODES = 8
PATCHES = 256
FRAMES = 16
EPS = 1e-06
BETA = 0.25
DP = ("dp_0", "dp_1")
TM = ("tm_0", "tm_1")
HALF = 512
EXTRA = 256
GRADS = 256
PIECES = 7
GROUPS = 4
ROWS = 512
BF = jnp.bfloat16
F32 = jnp.float32
HIGHEST = lax.Precision.HIGHEST


def params(mebibytes):
    return pltpu.CompilerParams(vmem_limit_bytes=mebibytes * 1024 * 1024)


SMEM = pl.BlockSpec(memory_space=pltpu.SMEM)


def nn(a, b, precision=None):
    return lax.dot_general(
        a, b, (((1,), (0,)), ((), ())), precision=precision, preferred_element_type=F32
    )


def nt(a, b, precision=None):
    return lax.dot_general(
        a, b, (((1,), (1,)), ((), ())), precision=precision, preferred_element_type=F32
    )


def tn(a, b, precision=None):
    return lax.dot_general(
        a, b, (((0,), (0,)), ((), ())), precision=precision, preferred_element_type=F32
    )


def two_terms(value):
    high = value.astype(BF)
    return high, (value - high.astype(F32)).astype(BF)


def iota(shape, dim):
    return lax.broadcasted_iota(jnp.int32, shape, dim)


def turned(value, shift):
    width = value.shape[-1]
    tiles = [pltpu.roll(value[:, j : j + 128], shift, 1) for j in range(0, width, 128)]
    return jnp.concatenate(tiles, axis=1)


def share_kernel(side_ref, weight_ref, out_ref, own_ref, sem):
    copies = []
    for part in range(3):
        at = pl.multiple_of(part * D + side_ref[0] * HALF, HALF)
        lanes = pl.ds(part * HALF, HALF)
        piece = weight_ref.at[:, pl.ds(at, HALF)]
        copies.append(pltpu.make_async_copy(piece, own_ref.at[:, lanes], sem.at[part]))
    for copy in copies:
        copy.start()
    for copy in copies:
        copy.wait()
    sends = [
        pltpu.make_async_copy(own_ref, out_ref.at[to], sem.at[3 + to])
        for to in range(out_ref.shape[0])
    ]
    for send in sends:
        send.start()
    for send in sends:
        send.wait()


def share(side, weight, count):
    rows = weight.shape[0]
    return pl.pallas_call(
        share_kernel,
        in_specs=[SMEM, pl.BlockSpec(memory_space=pl.ANY)],
        out_specs=pl.BlockSpec(memory_space=pl.ANY),
        out_shape=pltpu.HBM((count, rows, 3 * HALF), BF),
        scratch_shapes=[
            pltpu.VMEM((rows, 3 * HALF), BF),
            pltpu.SemaphoreType.DMA((3 + count,)),
        ],
        compiler_params=params(8),
        name="share",
    )(side, *in_hbm(weight))


def norm_kernel(code_ref, turn_ref, tokens_ref, gain_ref, normed_ref, extra_ref):
    xf = tokens_ref[...].astype(F32)
    scale = lax.rsqrt(jnp.mean(xf * xf, axis=-1, keepdims=True) + EPS)
    normed = xf * scale * gain_ref[...].astype(F32)
    normed_ref[...] = turned(normed, (128 - turn_ref[0]) % 128).astype(BF)
    mean = jnp.mean(xf, axis=0, keepdims=True)
    rows = jnp.concatenate([mean[:, j * 128 : (j + 1) * 128] for j in range(8)], axis=0)
    high = rows.astype(BF).astype(F32)
    mid = (rows - high).astype(BF).astype(F32)
    low = rows - high - mid
    code = jnp.full((8, 128), code_ref[0], jnp.int32).astype(F32)
    extra_ref[:, :128] = jnp.concatenate([high, mid], axis=0).astype(BF)
    extra_ref[:, 128:] = jnp.concatenate([low, code], axis=0).astype(BF)


def gathered(refs):
    own, *rest = refs
    half = rest[0].shape[0]
    after, across, before = (rest[i : i + 2] for i in range(0, 6, 2))
    rows = []
    for far in range(2 * half):
        part, at = (far // half, far % half)
        rows += [own[far], after[part][at], across[part][at], before[part][at]]
    return jnp.concatenate(rows, axis=0)


def grouped_rows(value):
    value = value.reshape(FRAMES, GROUPS, 8, value.shape[-1])
    return jnp.concatenate([value[:, g].reshape(128, -1) for g in range(GROUPS)], axis=0)


def frame_of(row):
    return row % 8 * 2 + row // 8


def causal_same_patch():
    row, col = (iota((128, 128), 0), iota((128, 128), 1))
    return (row % 8 == col % 8) & (frame_of(col // 8) <= frame_of(row // 8))


def head_masks():
    lane = iota((1, 128), 1)
    return tuple(jnp.where(lane // HEAD_DIM == j, 1.0, 0.0).astype(BF) for j in range(2))


def by_head(value, masks):
    return jnp.concatenate([value * mask for mask in masks], axis=0)


def units():
    return [(pair, group, pair * GROUPS + group) for pair in range(2) for group in range(GROUPS)]


def forward_heads(x_ref, weight_refs, qkv_ref, prob_ref):
    x = x_ref[...].reshape(ROWS, D)
    for part in range(3):
        weight = gathered(weight_refs[part * PIECES : (part + 1) * PIECES])
        qkv_ref[part] = grouped_rows(nn(x, weight)).astype(BF)
    allowed = causal_same_patch()
    masks = head_masks()

    def taken(part, pair, group):
        return qkv_ref[part, pl.ds(group * 128, 128), pl.ds(pair * 128, 128)]

    for pair, group, unit in units():
        scores = nt(by_head(taken(0, pair, group), masks), taken(1, pair, group))
        for j in range(2):
            one = scores[j * 128 : (j + 1) * 128] * HEAD_DIM ** (-0.5)
            prob_ref[unit * 2 + j] = jnp.where(allowed, one, -1e30)
    for at in range(16):
        scores = prob_ref[at]
        raised = jnp.exp(scores - jnp.max(scores, axis=1, keepdims=True))
        prob_ref[at] = raised * (1.0 / jnp.sum(raised, axis=1, keepdims=True))
    totals = [jnp.zeros((FRAMES, 128), F32)] * 2
    for pair, group, unit in units():
        weights = jnp.concatenate([prob_ref[unit * 2 + j] for j in range(2)], axis=1).astype(BF)
        mixed = nn(weights, by_head(taken(2, pair, group), masks))
        attended = mixed.astype(BF).astype(F32)
        totals[pair] = totals[pair] + jnp.sum(attended.reshape(FRAMES, 8, 128), axis=1)
    return jnp.concatenate(totals, axis=1)


def forward_kernel(_, __, side_ref, same_ref, cross_ref, *refs):
    extra_ref, qkv_ref, prob_ref, out_ref, x_ref, sum_ref = refs[3 * PIECES :]
    step = pl.program_id(0)

    @pl.when(step == 0)
    def _():
        x_ref[side_ref[0]] = same_ref[...]
        x_ref[1 - side_ref[0]] = cross_ref[...]

    lanes = pl.ds(pl.multiple_of(step * 256, 256), 256)
    sum_ref[:, lanes] = forward_heads(x_ref, refs[: 3 * PIECES], qkv_ref, prob_ref)

    @pl.when(step == 1)
    def _():
        sums = sum_ref[...].astype(BF)
        for to in range(FRAMES):
            out_ref[to, :, :HALF] = sums
            out_ref[to, :, HALF:] = extra_ref[...]


def weight_specs(weight):
    return [
        pl.BlockSpec((*piece.shape[:2], 256), lambda i, part=part: (0, 0, part * 2 + i))
        for part in range(3)
        for piece in weight
    ]


def whole(shape):
    return pl.BlockSpec(shape, lambda *_: (0,) * len(shape))


SAVED_SHAPES = (
    pltpu.HBM((3, ROWS, HALF), BF),
    pltpu.HBM((32, 128, 128), F32),
)


def saved_specs():
    return [
        pl.BlockSpec((3, ROWS, 256), lambda i: (0, 0, i)),
        pl.BlockSpec((16, 128, 128), lambda i: (i, 0, 0)),
    ]


def in_hbm(*values):
    return [pltpu.with_memory_space_constraint(v, pltpu.HBM) for v in values]


def forward(ready, ready_too, side, same, cross, weight, extra):
    return pl.pallas_call(
        forward_kernel,
        grid=(2,),
        in_specs=[
            *[pl.BlockSpec(memory_space=pl.ANY)] * 2,
            SMEM,
            whole(same.shape),
            whole(cross.shape),
            *weight_specs(weight),
            whole((16, EXTRA)),
        ],
        out_specs=[*saved_specs(), whole((16, 16, HALF + EXTRA))],
        out_shape=(*SAVED_SHAPES, pltpu.HBM((16, 16, HALF + EXTRA), BF)),
        scratch_shapes=[pltpu.VMEM((2, 8, 32, D), BF), pltpu.VMEM((FRAMES, HALF), F32)],
        compiler_params=params(24),
        cost_estimate=cost(1_000),
        name="forward",
    )(*in_hbm(ready, ready_too), side, same, cross, *weight * 3, extra)


def head_kernel(
    at_ref, got_ref, out_w_hbm, pair_hbm, book_ref, rows_ref, mean_ref, send_ref, *scratch
):
    pooled_ref, out_w_ref, pair_ref, sem = scratch
    copies = [
        pltpu.make_async_copy(out_w_hbm, out_w_ref, sem.at[0]),
        pltpu.make_async_copy(pair_hbm, pair_ref, sem.at[1]),
    ]
    for copy in copies:
        copy.start()
    got = got_ref[...].reshape(8, 2, 16, HALF + EXTRA)
    sums = [jnp.sum(got[:, c, :, :HALF].astype(F32), axis=0) for c in range(2)]
    sums = jnp.concatenate(sums, axis=1)
    got = got.reshape(16, 16, HALF + EXTRA)
    first = got[:, :, HALF : HALF + 128].reshape(256, 128)
    second = got[:, :, HALF + 128 :].reshape(256, 128)
    row, col = (iota((128, 256), 0), iota((128, 256), 1))
    frame, piece = (frame_of(row % 16), row // 16)
    same = col // 16 == frame
    pick_two = jnp.where(same & (col % 8 == piece), 1.0, 0.0).astype(BF)
    pick_one = jnp.where(same & (col % 16 == piece), 1.0, 0.0).astype(BF)
    means = nn(pick_two, first) + nn(pick_one, second)
    xmean = jnp.concatenate([means[j * 16 : (j + 1) * 16] for j in range(8)], axis=1)
    row, col = (iota((16, 256), 0), iota((16, 256), 1))
    pick_code = jnp.where(col == frame_of(row) * 16 + 8, 1.0, 0.0).astype(BF)
    code = nn(pick_code, second)
    for copy in copies:
        copy.wait()
    sums = jnp.concatenate(two_terms(sums), axis=0)
    moved = nn(sums, out_w_ref[...])
    pooled = xmean + (moved[:FRAMES] + moved[FRAMES:]) / PATCHES
    now = nt(pooled, pair_ref[0], HIGHEST)
    later = nt(pooled, pair_ref[1], HIGHEST)
    zero = jnp.zeros((1, LATENT), F32)
    action = now + jnp.concatenate([later[8:], later[1:8], zero], axis=0)
    quantized = jnp.zeros((FRAMES, LATENT), F32)
    for k in range(CODES):
        quantized = quantized + jnp.where(code[:, :LATENT] == k, book_ref[k : k + 1, :], 0.0)
    d_action = 2.0 * BETA * (action - quantized)
    d_before = jnp.concatenate([zero, d_action[8:15], d_action[:8]], axis=0)
    d_mean = nn(d_action, pair_ref[0], HIGHEST) + nn(d_before, pair_ref[1], HIGHEST)
    mean_ref[...] = d_mean
    terms = jnp.concatenate(two_terms(d_mean), axis=0)
    both = nt(terms, out_w_ref[...])
    rows_ref[...] = (both[:FRAMES] + both[FRAMES:]).astype(BF)
    pooled_ref[...] = pooled
    mine = pooled_ref[:, pl.ds(pl.multiple_of(at_ref[0] * 128, 128), 128)]
    high, low = two_terms(d_action)
    others = [mine.astype(BF), high, low, code[:, : 2 * LATENT].astype(BF)]
    mine = jnp.concatenate(others, axis=1)
    for to in range(send_ref.shape[0]):
        send_ref[to] = mine


def head(at, got, out_w, w_pair, codebook, clips):
    return pl.pallas_call(
        head_kernel,
        in_specs=[
            SMEM,
            pl.BlockSpec(memory_space=pltpu.VMEM),
            *[pl.BlockSpec(memory_space=pl.ANY)] * 2,
            pl.BlockSpec(memory_space=pltpu.VMEM),
        ],
        out_shape=(
            pltpu.HBM((FRAMES, D), BF),
            pltpu.HBM((FRAMES, D), F32),
            pltpu.HBM((clips, FRAMES, 256), BF),
        ),
        scratch_shapes=[
            pltpu.VMEM((FRAMES, D), F32),
            pltpu.VMEM((D, D), BF),
            pltpu.VMEM((2, LATENT, D), F32),
            pltpu.SemaphoreType.DMA((2,)),
        ],
        compiler_params=params(16),
        cost_estimate=cost(1_000),
        name="head",
    )(at, got, *in_hbm(out_w, w_pair), codebook)


def backward_heads(rows_ref, at, qkv_ref, prob_ref, weight_refs, acc_ref, cot_ref, part_ref):
    masks = head_masks()
    d_frames = rows_ref[:, pl.ds(at, 256)].astype(F32)
    d_all = jnp.broadcast_to(d_frames[:, None, :], (FRAMES, 8, 256)).reshape(128, 256).astype(BF)
    d_heads = [by_head(d_all[:, pair * 128 : (pair + 1) * 128], masks) for pair in range(2)]

    def taken(part, pair, group):
        return qkv_ref[part, pl.ds(group * 128, 128), pl.ds(pair * 128, 128)]

    for pair, group, unit in units():
        d_weights = nt(d_heads[pair], taken(2, pair, group))
        for j in range(2):
            cot_ref[unit * 2 + j] = d_weights[j * 128 : (j + 1) * 128].astype(BF)
    for index in range(16):
        prob = prob_ref[index]
        d_weights = cot_ref[index].astype(F32)
        inner = jnp.sum(d_weights * prob, axis=1, keepdims=True)
        cot_ref[index] = (prob * (d_weights - inner) * HEAD_DIM ** (-0.5)).astype(BF)
    for pair, group, unit in units():
        d_scores = [cot_ref[unit * 2 + j] for j in range(2)]
        prob = jnp.concatenate([prob_ref[unit * 2 + j].astype(BF) for j in range(2)], axis=0)
        d_query = nn(jnp.concatenate(d_scores, axis=1), by_head(taken(1, pair, group), masks))
        d_keys = tn(jnp.concatenate(d_scores, axis=0), by_head(taken(0, pair, group), masks))
        d_values = tn(prob, d_heads[pair])
        for part, value in enumerate((d_query, d_keys, d_values)):
            part_ref[part, pl.ds(group * 128, 128), pl.ds(pair * 128, 128)] = value.astype(BF)
    total = None
    for part in range(3):
        term = nt(part_ref[part], gathered(weight_refs[part * PIECES : (part + 1) * PIECES]))
        total = term if total is None else total + term
    acc_ref[...] += total


def backward_kernel(side_ref, rows_ref, *refs):
    keep_ref, give_ref, acc_ref, parts_ref, *scratch = refs[2 + 3 * PIECES :]
    step = pl.program_id(0)
    side = side_ref[0]

    @pl.when(step == 0)
    def _():
        acc_ref[...] = jnp.zeros_like(acc_ref)

    at = pl.multiple_of(side * HALF + step * 256, 256)
    backward_heads(rows_ref, at, refs[0], refs[1], refs[2 : 2 + 3 * PIECES], acc_ref, *scratch)

    @pl.when(step == 1)
    def _():
        for group in range(GROUPS):
            rows = acc_ref[pl.ds(group * 128, 128), :].reshape(2, 8, 8, D)
            parts_ref[:, :, pl.ds(group * 8, 8), :] = rows
        keep_ref[...] = parts_ref[side]
        give_ref[...] = parts_ref[1 - side].astype(BF)


def backward(side, d_rows, qkv, prob, weight):
    return pl.pallas_call(
        backward_kernel,
        grid=(2,),
        in_specs=[SMEM, whole((FRAMES, D)), *saved_specs(), *weight_specs(weight)],
        out_specs=[whole((8, 32, D))] * 2,
        out_shape=(pltpu.HBM((8, 32, D), F32), jax.ShapeDtypeStruct((8, 32, D), BF)),
        scratch_shapes=[
            pltpu.VMEM((ROWS, D), F32),
            pltpu.VMEM((2, 8, 32, D), F32),
            pltpu.VMEM((16, 128, 128), BF),
            pltpu.VMEM((3, ROWS, 256), BF),
        ],
        compiler_params=params(32),
        cost_estimate=cost(1_000),
        name="backward",
    )(side, *in_hbm(d_rows, qkv, prob), *weight * 3)


def grads_kernel(_, keep_ref, cross_ref, got_ref, out_ref, step_ref):
    count = got_ref.shape[0] * FRAMES
    got = got_ref[...].reshape(count, 256)
    means, others = (got[:, :128], got[:, 128:])
    wide = others.astype(F32)
    place, lane = (iota((count, 128), 0) % FRAMES, iota((count, 128), 1))
    shift = jnp.where(place == 0, 0.0, pltpu.roll(wide, count - 7, 0))
    before = jnp.where(place >= 8, pltpu.roll(wide, 8, 0), shift).astype(BF)
    code = wide[:, 2 * LATENT : 2 * LATENT + 1]
    onehot = jnp.where((code == lane.astype(F32)) & (lane < CODES), 1.0, 0.0).astype(BF)
    for part, value in enumerate((others, before)):
        terms = tn(value, means)
        total = (terms[:LATENT] + terms[LATENT : 2 * LATENT]).astype(BF)
        for to in range(8):
            out_ref[to, :, D + part * 128 : D + (part + 1) * 128] = total
    counted = jnp.where(lane < 2 * LATENT, wide, 1.0).astype(BF)
    totals = tn(onehot, counted)[:CODES]
    by_code = (totals[:, :LATENT] + totals[:, LATENT : 2 * LATENT]) * (-1.0 / BETA)
    out_ref[:, :, :D] = (keep_ref[...] + cross_ref[...].astype(F32)).astype(BF)
    step_ref[...] = by_code / totals[:, 2 * LATENT : 2 * LATENT + 1]


def grads(ready, keep, cross, got):
    return pl.pallas_call(
        grads_kernel,
        in_specs=[pl.BlockSpec(memory_space=pl.ANY), *[pl.BlockSpec(memory_space=pltpu.VMEM)] * 3],
        out_shape=(
            pltpu.HBM((8, 32, D + GRADS), BF),
            jax.ShapeDtypeStruct((CODES, LATENT), F32),
        ),
        compiler_params=params(8),
        cost_estimate=cost(1_000),
        name="grads",
    )(*in_hbm(ready), keep, cross, got)


def last_kernel(at_ref, turn_ref, got_ref, tokens_ref, gain_ref, mean_ref, out_ref, pair_ref):
    xf = tokens_ref[...].astype(F32)
    scale = lax.rsqrt(jnp.mean(xf * xf, axis=-1, keepdims=True) + EPS)
    d_normed = turned(got_ref[:, :, :D].reshape(xf.shape).astype(F32), turn_ref[0])
    d_scaled = d_normed * gain_ref[...].astype(F32)
    inner = jnp.sum(d_scaled * xf, axis=-1, keepdims=True) / D
    d_through = d_scaled * scale - xf * (scale * scale * scale * inner)
    d_resid = mean_ref[pl.ds(at_ref[0], 1), :]
    out_ref[...] = (d_resid + d_through).astype(BF)
    for t in range(2):
        for part in range(2):
            value = got_ref[t, :, pl.ds(D + part * 128, 128)]
            pair_ref[part, :, pl.ds(t * 128, 128)] = value.astype(F32)


def last(at, turn, got, tokens, gain, d_mean):
    return pl.pallas_call(
        last_kernel,
        grid=(4,),
        in_specs=[
            SMEM,
            SMEM,
            pl.BlockSpec((2, 32, D + GRADS), lambda i: (i, 0, 0)),
            pl.BlockSpec((64, D), lambda i: (i, 0)),
            whole((1, D)),
            whole((FRAMES, D)),
        ],
        out_specs=[
            pl.BlockSpec((64, D), lambda i: (i, 0)),
            pl.BlockSpec((2, LATENT, 256), lambda i: (0, 0, i)),
        ],
        out_shape=(
            jax.ShapeDtypeStruct((PATCHES, D), BF),
            jax.ShapeDtypeStruct((2, LATENT, D), F32),
        ),
        compiler_params=params(8),
        name="last",
    )(at, turn, got, tokens, gain, d_mean)


def cost(flops):
    return pl.CostEstimate(flops=flops, transcendentals=0, bytes_accessed=0)


def touch_kernel(*refs):
    refs[-1][...] = jnp.zeros_like(refs[-1])


def touched(flops, *values):
    return pl.pallas_call(
        touch_kernel,
        in_specs=[pl.BlockSpec(memory_space=pltpu.VMEM)] * len(values),
        out_shape=pltpu.HBM((8, 128), F32),
        compiler_params=params(4),
        cost_estimate=cost(flops),
        name="touch",
    )(*values)


def shifted(value, axis, by):
    count = lax.axis_size(axis)
    return lax.ppermute(value, axis, [(i, (i + by) % count) for i in range(count)])


def local(tokens, gain, w_qkv, w_out, w_pair, codebook, codes):
    side = lax.axis_index("tm_1")
    layer = lax.axis_index("tm_0")
    turn = (lax.axis_index("dp_1") * 32).reshape(1)
    rows = w_qkv.shape[0]
    tokens = tokens.reshape(PATCHES, D)
    gain = gain.reshape(1, D)
    full_out = lax.all_gather(w_out, DP, axis=0, tiled=True)
    far = lax.axis_size("dp_0")
    near = lax.all_to_all(share(side.reshape(1), w_qkv, far), "dp_0", 0, 0, tiled=True)
    half = near.shape[0] // 2
    early, late = (near[:half], near[half:])
    before_early = shifted(early, "dp_1", 1)
    after_late = shifted(late, "dp_1", -1)
    first = shifted(before_early, "dp_1", 1)
    second = shifted(after_late, "dp_1", -1)
    after = [shifted(early, "dp_1", -1), after_late]
    before = [before_early, shifted(late, "dp_1", 1)]
    own_w = [near, *after, first, second, *before]
    at = (side * 8 + layer).reshape(1)
    layer = layer.reshape(1)
    side = side.reshape(1)

    normed, extra = pl.pallas_call(
        norm_kernel,
        in_specs=[
            SMEM,
            SMEM,
            *[pl.BlockSpec(memory_space=pltpu.VMEM)] * 2,
        ],
        out_shape=(
            pltpu.HBM((PATCHES, D), BF),
            jax.ShapeDtypeStruct((16, EXTRA), BF),
        ),
        compiler_params=params(8),
        cost_estimate=cost(1_000),
        name="norm",
    )(codes.reshape(1), turn, tokens, gain)
    same = lax.all_to_all(normed.reshape(8, 32, D), "tm_0", 0, 0, tiled=True)
    cross = shifted(same, "tm_1", 1)
    qkv, prob, partial = forward(touched(10_000_000_000, first, second), touched(10_000_000_000, after[0], before[1]), side, same, cross, own_w, extra)
    arrived = lax.all_to_all(partial, TM, 0, 0, tiled=True)
    clips = lax.axis_size(DP)
    pair = jnp.swapaxes(w_pair, 1, 2)
    d_rows, d_mean, mine = head(layer, arrived, full_out, pair, codebook, clips)
    everyone = lax.all_to_all(mine, DP, 0, 0, tiled=True)
    keep, give = backward(side, d_rows, qkv, prob, own_w)
    ready = touched(1_000_000_000, everyone)
    outgoing, codebook_step = grads(ready, keep, shifted(give, "tm_1", 1), everyone)
    back = lax.all_to_all(outgoing, "tm_0", 0, 0, tiled=True)
    grad_tokens, grad_pair = last(at, turn, back, tokens, gain, d_mean)
    return (
        grad_tokens.reshape(1, 1, PATCHES, D),
        jnp.swapaxes(grad_pair, 1, 2),
        codebook_step,
    )


def solution(mesh):
    torus = Mesh(mesh.devices.reshape(8, 4, 8, 2), ("dp_0", "dp_1", "tm_0", "tm_1"))
    return jax.shard_map(
        local,
        mesh=torus,
        in_specs=(P(DP, TM, None, None), P(), P(DP, None), P(DP, None), P(), P(), P(DP, TM, None)),
        out_specs=(P(DP, TM, None, None), P(), P()),
        check_vma=False,
    )
```
